256 devices in a mesh: group: 8 (over z), row: 32 (over y, x, core).
Axes of the slice: x: 4, y: 4, z: 8, core: 2. Of those that a mesh axis runs over, the one named last changes fastest.
Arguments:
- start_basis: float32 [2048, 16, 128], P(('group', 'row')), may hold values from -6 to 6
- tiles: bfloat16 [2048, 16, 128, 128], P(('group', 'row')), may hold values from -60000 to 60000
- tile_cols: int32 [2048, 16], P(('group', 'row')), may hold values from 0 to 75, as said below
- tile_count: int32 [2048], P(('group', 'row')), may hold values from 10 to 16, as said below
- recv_list: int32 [8, 32, 32, 2], P('group', 'row'), may hold values from -1 to 2047, as said below
Outputs:
- krylov: float32 [3, 2048, 16, 128], P(None, ('group', 'row'))
The draws below stay inside these ranges and needn't reach their ends.
Inputs may be any that keep to these rules, and one draw needn't show every extreme that they name: For each reader device and each other device of its range, recv_list names distinct blocks of that peer in its first slots and -1 in the rest; a reader's own entry is all -1; every reader gets exactly 2 blocks from some peer. tile_cols never names an empty receive slot, nor a rim slot of a range that does not exist (before the first or after the last group); every filled receive slot and every existing rim slot is named by some tile slot below 10. `tile_count`: every device has a row block with all 16 tiles live.
All inputs are finite; a program needn't handle non-finite values.
Results may differ from the reference program's by a relative error of at most 0.0003.
Values sent between devices are 32-bit elements; how exact they have to be, the bound alone decides.
A program may use at most 64 MiB of HBM per device.

```python
import jax
import jax.numpy as jnp
from jax import lax

BLOCK = 128
VECS = 16
BLOCKS_DEV = 8
TILES_ROW = 16
SLOTS = 2
RIM = 2
ITERS = 3
GROUPS = 8
PEERS = 32
NBLOCKS = 2048
MINLIVE = 10


def layout(key):
    seeded = jax.random.fold_in(key, 101)
    key_need, key_perm, key_fill, key_count, key_top = jax.random.split(seeded, 5)
    peer_q = jnp.arange(PEERS)[:, None]
    peer_p = jnp.arange(PEERS)[None, :]
    distance = jnp.abs(peer_q - peer_p)
    rolled = jax.random.randint(key_need, (GROUPS, PEERS, PEERS), 0, 2 * SLOTS + 2)
    near_count = jnp.minimum(rolled, SLOTS)
    far_count = jnp.clip(rolled - SLOTS, 0, SLOTS)
    needed = jnp.where(distance[None] <= 4, near_count, far_count)
    needed = jnp.where(distance[None] == 1, SLOTS, needed)
    needed = jnp.where(distance[None] == 0, 0, needed)
    scores = jax.random.randint(key_perm, (GROUPS, PEERS, PEERS, BLOCKS_DEV), 0, 1 << 20) * BLOCKS_DEV + jnp.arange(BLOCKS_DEV)
    ranking = jnp.argsort(scores, axis=-1)[..., :SLOTS]
    slot_ids = jnp.arange(SLOTS)
    taken = slot_ids[None, None, None, :] < needed[..., None]
    owner_dev = jnp.arange(GROUPS)[:, None, None, None] * PEERS + jnp.arange(PEERS)[None, None, :, None]
    received = jnp.where(taken, owner_dev * BLOCKS_DEV + ranking, -1).astype(jnp.int32)
    group_ids = jnp.arange(GROUPS)[:, None, None]
    own_ok = jnp.ones((GROUPS, PEERS, BLOCKS_DEV), jnp.bool_)
    peer_ok = taken.reshape(GROUPS, PEERS, PEERS * SLOTS)
    lower_ok = jnp.broadcast_to(group_ids > 0, (GROUPS, PEERS, RIM))
    upper_ok = jnp.broadcast_to(group_ids < GROUPS - 1, (GROUPS, PEERS, RIM))
    usable = jnp.concatenate([own_ok, peer_ok, lower_ok, upper_ok], axis=-1)
    extent = BLOCKS_DEV + PEERS * SLOTS + 2 * RIM
    sort_keys = jnp.where(usable, 0, extent) + jnp.arange(extent)
    compact = jnp.argsort(sort_keys, axis=-1).astype(jnp.int32)
    usable_count = jnp.sum(usable, axis=-1).astype(jnp.int32)
    cover_rank = jnp.arange(TILES_ROW)[None, :] * BLOCKS_DEV + jnp.arange(BLOCKS_DEV)[:, None]
    covered = cover_rank[None, None] < usable_count[..., None, None]
    fill_pick = jax.random.randint(key_fill, (GROUPS, PEERS, BLOCKS_DEV, TILES_ROW), 0, 1 << 20) % usable_count[..., None, None]
    position = jnp.where(covered, cover_rank[None, None], fill_pick).reshape(GROUPS, PEERS, BLOCKS_DEV * TILES_ROW)
    columns = jnp.take_along_axis(compact, position, axis=-1).reshape(NBLOCKS, TILES_ROW).astype(jnp.int32)
    rolled_count = jax.random.randint(key_count, (GROUPS, PEERS, BLOCKS_DEV), MINLIVE, TILES_ROW + 1)
    top_block = jax.random.randint(key_top, (GROUPS, PEERS, 1), 0, BLOCKS_DEV)
    counts = jnp.where(jnp.arange(BLOCKS_DEV)[None, None, :] == top_block, TILES_ROW, rolled_count)
    return (received, columns, counts.reshape(NBLOCKS).astype(jnp.int32))


def draw_recv_list(key, part):
    return layout(key)[0]


def draw_tile_cols(key, part):
    return layout(key)[1]


def draw_tile_count(key, part):
    return layout(key)[2]


def draw_tiles(key, part):
    seeded = jax.random.fold_in(key, 202)
    key_values, key_rows, key_cols = jax.random.split(seeded, 3)
    shape = (NBLOCKS, TILES_ROW, BLOCK, BLOCK)
    values = jnp.clip(jax.random.normal(key_values, shape, jnp.float32), -6.0, 6.0)
    rising = 9.0 ** (jnp.arange(NBLOCKS, dtype=jnp.float32) / NBLOCKS)
    row_scale = jnp.exp(jax.random.uniform(key_rows, (NBLOCKS, 1, BLOCK, 1), jnp.float32, 0.0, 4.6))
    col_scale = jnp.exp(jax.random.uniform(key_cols, (NBLOCKS, TILES_ROW, 1, BLOCK), jnp.float32, 0.0, 2.3))
    return (values * rising[:, None, None, None] * row_scale * col_scale).astype(jnp.bfloat16)


def block_levels(stream_key, dims, shards, low, top_value):
    factor_of = 1.0
    for dim, shards_of in shards:
        draws = jax.random.uniform(jax.random.fold_in(jax.random.fold_in(stream_key, 6), dim), (shards_of,), jnp.float32, low / len(shards), top_value / len(shards))
        factor_of = factor_of * jnp.repeat(jnp.exp(draws), dims[dim] // shards_of).reshape((-1,) + (1,) * (len(dims) - 1 - dim))
    return factor_of


def noise(key, shape, scale, limit, shards=(), kind=jnp.bfloat16):
    result = scale * jax.random.normal(key, shape, jnp.float32)
    if shards:
        result = result * block_levels(key, shape, shards, -0.22, 0.18)
    return jnp.clip(result, -limit, limit).astype(kind)


def setup_inputs(seed: int = 0) -> dict:
    seeds = jax.random.split(jax.random.key(seed), 6)
    return {
        "start_basis": noise(seeds[0], (NBLOCKS, VECS, BLOCK), 1.0, 6.0, ((0, 256),), jnp.float32),
        "tiles": draw_tiles(jax.random.fold_in(seeds[5], 71), 0),
        "tile_cols": draw_tile_cols(jax.random.fold_in(seeds[5], 71), 0),
        "tile_count": draw_tile_count(jax.random.fold_in(seeds[5], 71), 0),
        "recv_list": draw_recv_list(jax.random.fold_in(seeds[5], 71), 0),
    }


def slot_table(recv_list):
    devices = GROUPS * PEERS
    dev_ids = jnp.arange(devices, dtype=jnp.int32)
    own_ids = dev_ids[:, None] * BLOCKS_DEV + jnp.arange(BLOCKS_DEV, dtype=jnp.int32)[None, :]
    peer_ids = recv_list.reshape(devices, PEERS * SLOTS).astype(jnp.int32)
    group_of = dev_ids // PEERS
    rim_steps = jnp.arange(RIM, dtype=jnp.int32)[None, :]
    lower_ids = jnp.where((group_of > 0)[:, None], (dev_ids[:, None] - PEERS) * BLOCKS_DEV + BLOCKS_DEV - RIM + rim_steps, -1)
    upper_ids = jnp.where((group_of < GROUPS - 1)[:, None], (dev_ids[:, None] + PEERS) * BLOCKS_DEV + rim_steps, -1)
    return jnp.concatenate([own_ids, peer_ids, lower_ids.astype(jnp.int32), upper_ids.astype(jnp.int32)], axis=1)

def apply_op(tiles, global_cols, live_mask, inv_root, basis):
    devices = GROUPS * PEERS
    scaled = basis * inv_root[:, None, :]
    padded = jnp.concatenate([scaled, jnp.zeros((1, VECS, BLOCK), jnp.float32)], axis=0)

    def one_device(operands):
        tile_set, columns, mask_set, root_set = operands
        picked = jnp.take(padded, columns, axis=0) * mask_set[:, :, None, None]
        applied = jnp.einsum('btij,btkj->bki', tile_set.astype(jnp.float32), picked, precision=lax.Precision.HIGHEST)
        return applied * root_set[:, None, :]
    shaped = (tiles.reshape(devices, BLOCKS_DEV, TILES_ROW, BLOCK, BLOCK), global_cols.reshape(devices, BLOCKS_DEV, TILES_ROW), live_mask.reshape(devices, BLOCKS_DEV, TILES_ROW), inv_root.reshape(devices, BLOCKS_DEV, BLOCK))
    return lax.map(one_device, shaped).reshape(NBLOCKS, VECS, BLOCK)

def orthonormal(applied, gram_sum):
    factor = jnp.linalg.cholesky(gram_sum / (NBLOCKS * BLOCK))
    inverse = lax.linalg.triangular_solve(factor, jnp.eye(VECS, dtype=jnp.float32), left_side=True, lower=True)
    return jnp.einsum('kl,bli->bki', inverse, applied, precision=lax.Precision.HIGHEST)

def reference(start_basis, tiles, tile_cols, tile_count, recv_list):
    devices = GROUPS * PEERS
    live_mask = (jnp.arange(TILES_ROW, dtype=jnp.int32)[None, :] < tile_count[:, None]).astype(jnp.float32)

    def squares(operands):
        tile_set, mask_set = operands
        wide_tiles = tile_set.astype(jnp.float32)
        return jnp.einsum('btij,bt->bi', wide_tiles * wide_tiles, mask_set, precision=lax.Precision.HIGHEST)
    sum_sq = lax.map(squares, (tiles.reshape(devices, BLOCKS_DEV, TILES_ROW, BLOCK, BLOCK), live_mask.reshape(devices, BLOCKS_DEV, TILES_ROW))).reshape(NBLOCKS, BLOCK)
    inv_root = (1e-06 + sum_sq) ** (-0.25)
    table = slot_table(recv_list)
    dev_of_block = jnp.arange(NBLOCKS, dtype=jnp.int32) // BLOCKS_DEV
    global_cols = jnp.take_along_axis(table[dev_of_block], tile_cols.astype(jnp.int32), axis=1)
    global_cols = jnp.where(global_cols < 0, NBLOCKS, global_cols).astype(jnp.int32)
    basis = start_basis
    results = []
    for step_at in range(ITERS):
        applied = apply_op(tiles, global_cols, live_mask, inv_root, basis)
        gram_sum = jnp.einsum('bki,bli->kl', applied, applied, precision=lax.Precision.HIGHEST)
        basis = orthonormal(applied, gram_sum)
        results.append(basis)
    return jnp.stack(results)
```

```python
import functools

import jax
import jax.numpy as jnp
from jax import lax
from jax.experimental import pallas as pl
from jax.experimental.pallas import tpu as pltpu
from jax.sharding import PartitionSpec as P

SLOTS = 2
RIM = 2
ITERS = 3
MINLIVE = 10
MESH = pl.DeviceIdType.MESH
F32 = jnp.float32
BF16 = jnp.bfloat16
HIGHEST = lax.Precision.HIGHEST
NT = (((1,), (1,)), ((), ()))


def split(x):
    high = x.astype(BF16)
    return high, (x - high.astype(F32)).astype(BF16)


def kernel(
    groups,
    peers,
    cols,
    count,
    wanted,
    basis,
    tiles_hbm,
    out,
    tiles,
    inv_root,
    applied,
    own_0,
    own_1,
    own_2,
    stage,
    recv_0,
    recv_1,
    recv_2,
    rim,
    pieces,
    table,
    table_s,
    gram_near_0,
    gram_near_1,
    gram_near_2,
    gram_far_0,
    gram_far_1,
    gram_far_2,
    tile_sem,
    table_sem,
    list_sem,
    send_sem,
    recv_sem,
    rim_send,
    rim_recv,
    near_send,
    near_recv,
    far_send,
    far_recv,
):
    blocks, vectors, side = basis.shape
    per_row = cols.shape[1]
    own = (own_0, own_1, own_2)
    recv = (recv_0, recv_1, recv_2)
    gram_near = (gram_near_0, gram_near_1, gram_near_2)
    gram_far = (gram_far_0, gram_far_1, gram_far_2)
    group = lax.axis_index("group")
    me = lax.axis_index("row")
    up = lax.rem(group + 1, groups)
    down = lax.rem(group + groups - 1, groups)
    zero_slot = blocks + SLOTS * peers + 2 * RIM

    def peer(step):
        return lax.rem(me + step, peers)

    def far_peer(step):
        return lax.rem(group + step, groups)

    def copy_in(b):
        return pltpu.make_async_copy(tiles_hbm.at[b], tiles.at[b], tile_sem.at[b])

    for b in range(blocks):
        copy_in(b).start()

    barrier = pltpu.get_barrier_semaphore()

    @pl.loop(1, peers)
    def _(step):
        pl.semaphore_signal(barrier, inc=1, device_id=(group, peer(step)), device_id_type=MESH)

    @pl.loop(1, groups)
    def _(step):
        pl.semaphore_signal(barrier, inc=1, device_id=(far_peer(step), me), device_id_type=MESH)

    pl.semaphore_wait(barrier, peers - 1 + groups - 1)

    @pl.loop(1, peers)
    def _(step):
        pltpu.make_async_remote_copy(
            src_ref=wanted,
            dst_ref=table.at[me],
            send_sem=list_sem.at[0],
            recv_sem=list_sem.at[1],
            device_id=(group, peer(step)),
            device_id_type=MESH,
        ).start()

    ones = jnp.ones((vectors, 2 * side), BF16)

    @pl.loop(0, blocks)
    def _(b):
        copy_in(b).wait()
        live = count[b]
        total = jnp.zeros((side, side), F32)
        for s in range(per_row):
            wide = tiles[b, s].astype(F32)
            square = wide * wide
            if s >= MINLIVE:
                square = square * jnp.where(s < live, 1.0, 0.0).astype(F32)
            total = total + square
        sums = lax.dot_general(
            ones, jnp.concatenate(split(total), axis=1), NT, preferred_element_type=F32
        )
        root = 1.0 / jnp.sqrt(jnp.sqrt(1e-06 + sums))
        inv_root[b] = root
        own_0[b] = basis[b] * root

    def list_wait(ref, sem):
        return pltpu.make_async_copy(ref, ref, sem)

    part = table.at[pl.ds(0, peers - 1)]
    list_wait(part, list_sem.at[0]).wait()
    list_wait(part, list_sem.at[1]).wait()
    to_scalar = pltpu.make_async_copy(table, table_s, table_sem)
    to_scalar.start()
    to_scalar.wait()

    first_block = (group * peers + me) * blocks

    def send(t):
        source = own[t]
        for at, (lo, target) in enumerate(((blocks - RIM, up), (0, down))):
            pltpu.make_async_remote_copy(
                src_ref=source.at[pl.ds(lo, RIM)],
                dst_ref=rim.at[t, at],
                send_sem=rim_send.at[t, at],
                recv_sem=rim_recv.at[t, at],
                device_id=(target, me),
                device_id_type=MESH,
            ).start()

        @pl.loop(1, peers)
        def _(step):
            q = peer(step)
            for c in range(SLOTS):
                pick = jnp.clip(table_s[q, c, me] - first_block, 0, blocks - 1)
                stage[t, q, c] = source[pick]
            pltpu.make_async_remote_copy(
                src_ref=stage.at[t, q],
                dst_ref=recv[t].at[me],
                send_sem=send_sem.at[t],
                recv_sem=recv_sem.at[t],
                device_id=(group, q),
                device_id_type=MESH,
            ).start()

    def wait_recv(t):
        part = recv[t].at[pl.ds(0, peers - 1)]
        list_wait(part, recv_sem.at[t]).wait()
        for at in range(2):
            list_wait(rim.at[t, at], rim_recv.at[t, at]).wait()

    def put_pieces(at, value):
        high, low = split(value)
        pieces[pl.ds(at, value.shape[0]), 0:vectors] = high
        pieces[pl.ds(at, value.shape[0]), vectors : 2 * vectors] = low

    def multiply(t):
        put_pieces(0, own[t][...])

        @pl.loop(0, peers)
        def _(q):
            put_pieces(blocks + SLOTS * q, recv[t][q])

        for at in range(2):
            put_pieces(blocks + SLOTS * peers + RIM * at, rim[t, at])

        @pl.loop(0, blocks)
        def _(b):
            live = count[b]
            picked = []
            for s in range(per_row):
                slot = cols[b, s]
                if s >= MINLIVE:
                    slot = jnp.where(s < live, slot, zero_slot)
                picked.append(pieces[slot])
            both = lax.dot_general(
                jnp.concatenate(picked, axis=1),
                jnp.concatenate([tiles[b, s] for s in range(per_row)], axis=1),
                NT,
                preferred_element_type=F32,
            )
            applied[b] = (both[:vectors] + both[vectors:]) * inv_root[b]

    def wide(ref):
        return jnp.concatenate([ref[b] for b in range(blocks)], axis=1)

    row_of = lax.broadcasted_iota(jnp.int32, (vectors, side), 0)
    lane_of = lax.broadcasted_iota(jnp.int32, (vectors, side), 1)
    own_lane = lax.rem(row_of, 8) == lane_of // vectors
    row_total = groups * peers * blocks * side

    def gram_start(t, value):
        gram = lax.dot_general(
            value,
            jnp.concatenate([value] * (side // vectors), axis=0),
            NT,
            precision=HIGHEST,
            preferred_element_type=F32,
        )
        packed = jnp.sum(jnp.where(own_lane, gram, 0.0).reshape(vectors // 8, 8, side), axis=1)
        gram_near[t][me] = packed

        @pl.loop(1, peers)
        def _(step):
            pltpu.make_async_remote_copy(
                src_ref=gram_near[t].at[me],
                dst_ref=gram_near[t].at[me],
                send_sem=near_send.at[t],
                recv_sem=near_recv.at[t],
                device_id=(group, peer(step)),
                device_id_type=MESH,
            ).start()

    def gram_far_start(t):
        list_wait(gram_near[t].at[pl.ds(0, peers - 1)], near_recv.at[t]).wait()
        gram_far[t][group] = jnp.sum(gram_near[t][...], axis=0)

        @pl.loop(1, groups)
        def _(step):
            pltpu.make_async_remote_copy(
                src_ref=gram_far[t].at[group],
                dst_ref=gram_far[t].at[group],
                send_sem=far_send.at[t],
                recv_sem=far_recv.at[t],
                device_id=(far_peer(step), me),
                device_id_type=MESH,
            ).start()

    def gram_end(t):
        list_wait(gram_far[t].at[pl.ds(0, groups - 1)], far_recv.at[t]).wait()
        packed = jnp.sum(gram_far[t][...], axis=0) / row_total
        rows = jnp.broadcast_to(packed[:, None, :], (vectors // 8, 8, side)).reshape(vectors, side)
        full = jnp.where(own_lane, rows, 0.0)
        for shift in (64, 32, 16):
            full = full + pltpu.roll(full, shift, 1)
        both = jnp.where(lane_of < vectors, jnp.where(lane_of == row_of, 1.0, 0.0), full)
        pivots = jnp.zeros((vectors, side), F32)
        for j in range(vectors):
            pivot_row = jnp.broadcast_to(both[j : j + 1], (vectors, side))
            column = jnp.broadcast_to(both[:, vectors + j : vectors + j + 1], (vectors, side))
            pivot = jnp.broadcast_to(pivot_row[:, vectors + j : vectors + j + 1], (vectors, side))
            pivots = jnp.where(row_of == j, pivot, pivots)
            both = jnp.where(row_of > j, both - (column / pivot) * pivot_row, both)
        return (both / jnp.sqrt(pivots))[:, :vectors]

    def normalise(inverse, value):
        return lax.dot_general(
            inverse,
            value,
            (((1,), (0,)), ((), ())),
            precision=HIGHEST,
            preferred_element_type=F32,
        )

    def store_out(t, value):
        for b in range(blocks):
            out[t, b] = value[:, b * side : (b + 1) * side]

    pieces[zero_slot] = jnp.zeros((2 * vectors, side), BF16)
    send(0)
    wait_recv(0)
    multiply(0)
    current = wide(applied)
    for t in range(ITERS):
        if t + 1 < ITERS:
            for b in range(blocks):
                own[t + 1][b] = current[:, b * side : (b + 1) * side] * inv_root[b]
        gram_start(t, current)
        if t + 1 < ITERS:
            send(t + 1)
        gram_far_start(t)
        inverse = gram_end(t)
        store_out(t, normalise(inverse, current))
        if t + 1 < ITERS:
            wait_recv(t + 1)
            multiply(t + 1)
            current = normalise(inverse, wide(applied))

    for t in range(ITERS):
        list_wait(stage.at[t, pl.ds(0, peers - 1)], send_sem.at[t]).wait()
        for at in range(2):
            list_wait(rim.at[t, at], rim_send.at[t, at]).wait()
        list_wait(gram_near[t].at[pl.ds(0, peers - 1)], near_send.at[t]).wait()
        list_wait(gram_far[t].at[pl.ds(0, groups - 1)], far_send.at[t]).wait()


def local(groups, peers, start_basis, tiles, tile_cols, tile_count, recv_list):
    blocks, per_row, side, _ = tiles.shape
    vectors = start_basis.shape[1]
    wanted = jnp.transpose(recv_list.reshape(peers, SLOTS))
    slots = blocks + SLOTS * peers + 2 * RIM + 1
    dma = pltpu.SemaphoreType.DMA
    vmem = pltpu.VMEM
    smem = pl.BlockSpec(memory_space=pltpu.SMEM)
    near = vmem((peers, vectors // 8, side), F32)
    far = vmem((groups, vectors // 8, side), F32)
    return pl.pallas_call(
        functools.partial(kernel, groups, peers),
        out_shape=jax.ShapeDtypeStruct((ITERS, blocks, vectors, side), F32),
        in_specs=[
            smem,
            smem,
            pl.BlockSpec(memory_space=pltpu.VMEM),
            pl.BlockSpec(memory_space=pltpu.VMEM),
            pl.BlockSpec(memory_space=pl.ANY),
        ],
        out_specs=pl.BlockSpec(memory_space=pltpu.VMEM),
        scratch_shapes=[
            vmem((blocks, per_row, side, side), BF16),
            vmem((blocks, vectors, side), F32),
            vmem((blocks, vectors, side), F32),
        ]
        + [vmem((blocks, vectors, side), F32)] * ITERS
        + [vmem((ITERS, peers, SLOTS, vectors, side), F32)]
        + [vmem((peers, SLOTS, vectors, side), F32)] * ITERS
        + [
            vmem((ITERS, 2, RIM, vectors, side), F32),
            vmem((slots, 2 * vectors, side), BF16),
            vmem((peers, SLOTS, peers), jnp.int32),
            pltpu.SMEM((peers, SLOTS, peers), jnp.int32),
        ]
        + [near] * ITERS
        + [far] * ITERS
        + [
            dma((blocks,)),
            dma,
            dma((2,)),
            dma((ITERS,)),
            dma((ITERS,)),
            dma((ITERS, 2)),
            dma((ITERS, 2)),
            dma((ITERS,)),
            dma((ITERS,)),
            dma((ITERS,)),
            dma((ITERS,)),
        ],
        compiler_params=pltpu.CompilerParams(
            collective_id=0, has_side_effects=True, vmem_limit_bytes=40 << 20
        ),
    )(tile_cols, tile_count, wanted, start_basis, tiles)


def solution(mesh):
    placed = (
        P(("group", "row"), None, None),
        P(("group", "row"), None, None, None),
        P(("group", "row"), None),
        P(("group", "row")),
        P("group", "row", None, None),
    )
    return jax.shard_map(
        functools.partial(local, mesh.shape["group"], mesh.shape["row"]),
        mesh=mesh,
        in_specs=placed,
        out_specs=P(None, ("group", "row"), None, None),
        check_vma=False,
    )
```

```python
import functools

import jax
import jax.numpy as jnp
from jax import lax
from jax.experimental import pallas as pl
from jax.experimental.pallas import tpu as pltpu
from jax.sharding import PartitionSpec as P

SLOTS = 2
RIM = 2
ITERS = 3
MINLIVE = 10
PIECES = 3
UNROLL = 4
MESH = pl.DeviceIdType.MESH
F32 = jnp.float32
BF16 = jnp.bfloat16
HIGHEST = lax.Precision.HIGHEST
NT = (((1,), (1,)), ((), ()))


def split(x, count):
    parts = []
    for _ in range(count):
        parts.append(x.astype(BF16))
        x = x - parts[-1].astype(F32)
    return parts


def send_order(peers):
    far = [(2, 2), (1, 2), (2, 1), (3, 2), (2, 3), (1, 1), (3, 3), (1, 3), (3, 1)]
    near = [(2, 0), (0, 2), (1, 0), (0, 1), (3, 0), (0, 3)]
    order = [(y, x, c) for y, x in far + near for c in (0, 1)] + [(0, 0, 1)]
    if peers != 32:
        order = [(0, 0, step) for step in range(1, peers)]
    return order


def kernel(
    groups,
    peers,
    cols_hbm,
    count_hbm,
    wanted_hbm,
    basis_hbm,
    tiles_hbm,
    out,
    cols,
    count,
    wanted,
    basis,
    tiles,
    inv_root,
    applied,
    own_0,
    own_1,
    own_2,
    stage,
    recv_0,
    recv_1,
    recv_2,
    rim,
    pieces,
    table,
    table_s,
    gram_near_0,
    gram_near_1,
    gram_near_2,
    gram_far_0,
    gram_far_1,
    gram_far_2,
    tile_sem,
    list_sem,
    send_sem,
    recv_sem,
    rim_send,
    rim_recv,
    near_send,
    near_recv,
    far_send,
    far_recv,
    arg_sem,
):
    blocks, vectors, side = basis.shape
    per_row = cols.shape[1]
    own = (own_0, own_1, own_2)
    recv = (recv_0, recv_1, recv_2)
    gram_near = (gram_near_0, gram_near_1, gram_near_2)
    gram_far = (gram_far_0, gram_far_1, gram_far_2)
    group = lax.axis_index("group")
    me = lax.axis_index("row")
    up = lax.rem(group + 1, groups)
    down = lax.rem(group + groups - 1, groups)
    zero_slot = blocks + SLOTS * peers + 2 * RIM

    def peer(step):
        return lax.rem(me + step, peers)

    def offset_peer(offset):
        dy, dx, dc = offset
        if peers != 32:
            return peer(dc)
        y, x, c = me // 8, lax.rem(me // 2, 4), lax.rem(me, 2)
        return lax.rem(y + dy, 4) * 8 + lax.rem(x + dx, 4) * 2 + lax.rem(c + dc, 2)

    def far_peer(step):
        return lax.rem(group + step, groups)

    def copy_in(b):
        return pltpu.make_async_copy(tiles_hbm.at[b], tiles.at[b], tile_sem.at[b])

    arguments = [
        pltpu.make_async_copy(source, target, arg_sem.at[i])
        for i, (source, target) in enumerate(
            (
                (wanted_hbm, wanted),
                (count_hbm, count),
                (basis_hbm, basis),
                (cols_hbm, cols),
            )
        )
    ]
    for copy in arguments:
        copy.start()
    for b in range(blocks):
        copy_in(b).start()

    barrier = pltpu.get_barrier_semaphore()

    @pl.loop(1, peers)
    def _(step):
        pl.semaphore_signal(barrier, inc=1, device_id=(group, peer(step)), device_id_type=MESH)

    @pl.loop(1, groups)
    def _(step):
        pl.semaphore_signal(barrier, inc=1, device_id=(far_peer(step), me), device_id_type=MESH)

    for copy in arguments:
        copy.wait()
    pl.semaphore_wait(barrier, peers - 1 + groups - 1)

    @pl.loop(1, peers)
    def _(step):
        pltpu.make_async_remote_copy(
            src_ref=wanted,
            dst_ref=table.at[me],
            send_sem=list_sem.at[0],
            recv_sem=list_sem.at[1],
            device_id=(group, peer(step)),
            device_id_type=MESH,
        ).start()

    ones = jnp.ones((vectors, 3 * side), BF16)

    @pl.loop(0, blocks)
    def _(b):
        copy_in(b).wait()
        live = count[b]
        total = jnp.zeros((side, side), F32)
        for s in range(per_row):
            wide = tiles[b, s].astype(F32)
            square = wide * wide
            if s >= MINLIVE:
                square = square * jnp.where(s < live, 1.0, 0.0).astype(F32)
            total = total + square
        sums = lax.dot_general(
            ones, jnp.concatenate(split(total, 3), axis=1), NT, preferred_element_type=F32
        )
        root = 1.0 / jnp.sqrt(jnp.sqrt(1e-06 + sums))
        inv_root[b] = root
        own_0[b] = basis[b] * root

    def list_wait(ref, sem):
        return pltpu.make_async_copy(ref, ref, sem)

    part = table.at[pl.ds(0, peers - 1)]
    list_wait(part, list_sem.at[0]).wait()
    list_wait(part, list_sem.at[1]).wait()
    to_scalar = pltpu.make_async_copy(table, table_s, arg_sem.at[0])
    to_scalar.start()
    to_scalar.wait()

    first_block = (group * peers + me) * blocks

    def send(t):
        source = own[t]
        for at, (lo, target) in enumerate(((blocks - RIM, up), (0, down))):
            pltpu.make_async_remote_copy(
                src_ref=source.at[pl.ds(lo, RIM)],
                dst_ref=rim.at[t, at],
                send_sem=rim_send.at[t, at],
                recv_sem=rim_recv.at[t, at],
                device_id=(target, me),
                device_id_type=MESH,
            ).start()

        for offset in send_order(peers):
            q = offset_peer(offset)
            for c in range(SLOTS):
                pick = jnp.clip(table_s[q, c, me] - first_block, 0, blocks - 1)
                stage[t, q, c] = source[pick]
            pltpu.make_async_remote_copy(
                src_ref=stage.at[t, q],
                dst_ref=recv[t].at[me],
                send_sem=send_sem.at[t],
                recv_sem=recv_sem.at[t],
                device_id=(group, q),
                device_id_type=MESH,
            ).start()

    def wait_recv(t):
        part = recv[t].at[pl.ds(0, peers - 1)]
        list_wait(part, recv_sem.at[t]).wait()
        for at in range(2):
            list_wait(rim.at[t, at], rim_recv.at[t, at]).wait()

    def put_pieces(at, value):
        for i, part in enumerate(split(value, PIECES)):
            pieces[pl.ds(at, value.shape[0]), i * vectors : (i + 1) * vectors] = part

    def multiply(t):
        put_pieces(0, own[t][...])

        @pl.loop(0, peers)
        def _(q):
            put_pieces(blocks + SLOTS * q, recv[t][q])

        for at in range(2):
            put_pieces(blocks + SLOTS * peers + RIM * at, rim[t, at])

        @pl.loop(0, blocks, unroll=UNROLL)
        def _(b):
            live = count[b]
            picked = []
            for s in range(per_row):
                slot = cols[b, s]
                if s >= MINLIVE:
                    slot = jnp.where(s < live, slot, zero_slot)
                picked.append(pieces[slot])
            both = lax.dot_general(
                jnp.concatenate(picked, axis=1),
                jnp.concatenate([tiles[b, s] for s in range(per_row)], axis=1),
                NT,
                preferred_element_type=F32,
            )
            product = both[:vectors]
            for i in range(1, PIECES):
                product = product + both[i * vectors : (i + 1) * vectors]
            applied[b] = product * inv_root[b]

    def wide(ref):
        return jnp.concatenate([ref[b] for b in range(blocks)], axis=1)

    row_of = lax.broadcasted_iota(jnp.int32, (vectors, side), 0)
    lane_of = lax.broadcasted_iota(jnp.int32, (vectors, side), 1)
    own_lane = lax.rem(row_of, 8) == lane_of // vectors
    row_total = groups * peers * blocks * side

    def gram_start(t, value):
        gram = lax.dot_general(
            value,
            jnp.concatenate([value] * (side // vectors), axis=0),
            NT,
            precision=HIGHEST,
            preferred_element_type=F32,
        )
        packed = jnp.sum(jnp.where(own_lane, gram, 0.0).reshape(vectors // 8, 8, side), axis=1)
        gram_near[t][me] = packed

        @pl.loop(1, peers)
        def _(step):
            pltpu.make_async_remote_copy(
                src_ref=gram_near[t].at[me],
                dst_ref=gram_near[t].at[me],
                send_sem=near_send.at[t],
                recv_sem=near_recv.at[t],
                device_id=(group, peer(step)),
                device_id_type=MESH,
            ).start()

    def gram_far_start(t):
        list_wait(gram_near[t].at[pl.ds(0, peers - 1)], near_recv.at[t]).wait()
        gram_far[t][group] = jnp.sum(gram_near[t][...], axis=0)

        @pl.loop(1, groups)
        def _(step):
            pltpu.make_async_remote_copy(
                src_ref=gram_far[t].at[group],
                dst_ref=gram_far[t].at[group],
                send_sem=far_send.at[t],
                recv_sem=far_recv.at[t],
                device_id=(far_peer(step), me),
                device_id_type=MESH,
            ).start()

    def gram_end(t):
        list_wait(gram_far[t].at[pl.ds(0, groups - 1)], far_recv.at[t]).wait()
        packed = jnp.sum(gram_far[t][...], axis=0) / row_total
        rows = jnp.broadcast_to(packed[:, None, :], (vectors // 8, 8, side)).reshape(vectors, side)
        full = jnp.where(own_lane, rows, 0.0)
        for shift in (64, 32, 16):
            full = full + pltpu.roll(full, shift, 1)
        columns = [
            jnp.broadcast_to(full[:, k : k + 1], (vectors, side)) for k in range(vectors)
        ]
        inverse = jnp.where(lane_of == row_of, 1.0, 0.0).astype(F32)
        pivots = jnp.zeros((vectors, side), F32)

        def row(value, j):
            return jnp.broadcast_to(value[j : j + 1], (vectors, side))

        for j in range(vectors):
            pivot = row(columns[j], j)
            pivots = jnp.where(row_of == j, pivot, pivots)
            factor = jnp.where(row_of > j, columns[j] / pivot, 0.0)
            inverse = inverse - factor * row(inverse, j)
            for k in range(j + 1, vectors):
                columns[k] = columns[k] - factor * row(columns[k], j)
        return (inverse / jnp.sqrt(pivots))[:, :vectors]

    def normalise(inverse, value):
        return lax.dot_general(
            inverse,
            value,
            (((1,), (0,)), ((), ())),
            precision=HIGHEST,
            preferred_element_type=F32,
        )

    def store_out(t, value):
        for b in range(blocks):
            out[t, b] = value[:, b * side : (b + 1) * side]

    pieces[zero_slot] = jnp.zeros((PIECES * vectors, side), BF16)
    def spread(value, target):
        for b in range(blocks):
            target[b] = value[:, b * side : (b + 1) * side] * inv_root[b]

    send(0)
    wait_recv(0)
    multiply(0)
    first = wide(applied)
    spread(first, own_1)
    gram_start(0, first)
    send(1)
    gram_far_start(0)
    wait_recv(1)
    multiply(1)
    second = wide(applied)
    spread(second, own_2)
    gram_start(1, second)
    send(2)
    store_out(0, normalise(gram_end(0), first))
    gram_far_start(1)
    wait_recv(2)
    multiply(2)
    inverse = gram_end(1)
    third = normalise(inverse, wide(applied))
    gram_start(2, third)
    store_out(1, normalise(inverse, second))
    gram_far_start(2)
    store_out(2, normalise(gram_end(2), third))

    for t in range(ITERS):
        list_wait(stage.at[t, pl.ds(0, peers - 1)], send_sem.at[t]).wait()
        for at in range(2):
            list_wait(rim.at[t, at], rim_send.at[t, at]).wait()
        list_wait(gram_near[t].at[pl.ds(0, peers - 1)], near_send.at[t]).wait()
        list_wait(gram_far[t].at[pl.ds(0, groups - 1)], far_send.at[t]).wait()


def local(groups, peers, start_basis, tiles, tile_cols, tile_count, recv_list):
    blocks, per_row, side, _ = tiles.shape
    vectors = start_basis.shape[1]
    wanted = jnp.transpose(recv_list.reshape(peers, SLOTS))
    slots = blocks + SLOTS * peers + 2 * RIM + 1
    dma = pltpu.SemaphoreType.DMA
    vmem = pltpu.VMEM
    near = vmem((peers, vectors // 8, side), F32)
    far = vmem((groups, vectors // 8, side), F32)
    return pl.pallas_call(
        functools.partial(kernel, groups, peers),
        out_shape=jax.ShapeDtypeStruct((ITERS, blocks, vectors, side), F32),
        in_specs=[pl.BlockSpec(memory_space=pltpu.HBM)] * 5,
        out_specs=pl.BlockSpec(memory_space=pltpu.VMEM),
        scratch_shapes=[
            pltpu.SMEM(tile_cols.shape, jnp.int32),
            pltpu.SMEM(tile_count.shape, jnp.int32),
            vmem(wanted.shape, jnp.int32),
            vmem((blocks, vectors, side), F32),
            vmem((blocks, per_row, side, side), BF16),
            vmem((blocks, vectors, side), F32),
            vmem((blocks, vectors, side), F32),
        ]
        + [vmem((blocks, vectors, side), F32)] * ITERS
        + [vmem((ITERS, peers, SLOTS, vectors, side), F32)]
        + [vmem((peers, SLOTS, vectors, side), F32)] * ITERS
        + [
            vmem((ITERS, 2, RIM, vectors, side), F32),
            vmem((slots, PIECES * vectors, side), BF16),
            vmem((peers, SLOTS, peers), jnp.int32),
            pltpu.SMEM((peers, SLOTS, peers), jnp.int32),
        ]
        + [near] * ITERS
        + [far] * ITERS
        + [
            dma((blocks,)),
            dma((2,)),
            dma((ITERS,)),
            dma((ITERS,)),
            dma((ITERS, 2)),
            dma((ITERS, 2)),
            dma((ITERS,)),
            dma((ITERS,)),
            dma((ITERS,)),
            dma((ITERS,)),
            dma((4,)),
        ],
        compiler_params=pltpu.CompilerParams(
            collective_id=0, has_side_effects=True, vmem_limit_bytes=60 << 20
        ),
    )(tile_cols, tile_count, wanted, start_basis, tiles)


def solution(mesh):
    placed = (
        P(("group", "row"), None, None),
        P(("group", "row"), None, None, None),
        P(("group", "row"), None),
        P(("group", "row")),
        P("group", "row", None, None),
    )
    return jax.shard_map(
        functools.partial(local, mesh.shape["group"], mesh.shape["row"]),
        mesh=mesh,
        in_specs=placed,
        out_specs=P(None, ("group", "row"), None, None),
        check_vma=False,
    )
```

```python
import functools

import jax
import jax.numpy as jnp
from jax import lax
from jax.experimental import pallas as pl
from jax.experimental.pallas import tpu as pltpu
from jax.sharding import PartitionSpec as P

SLOTS = 2
RIM = 2
ITERS = 3
MINLIVE = 10
HALVES = 2
UNROLL = 8
UNROLL_PIECES = 8
MESH = pl.DeviceIdType.MESH
F32 = jnp.float32
BF16 = jnp.bfloat16
HIGHEST = lax.Precision.HIGHEST
NT = (((1,), (1,)), ((), ()))


def split(x, count):
    parts = []
    for _ in range(count):
        parts.append(x.astype(BF16))
        x = x - parts[-1].astype(F32)
    return parts


def send_order(peers):
    far = [(2, 2), (1, 2), (2, 1), (3, 2), (2, 3), (1, 1), (3, 3), (1, 3), (3, 1)]
    near = [(2, 0), (0, 2), (1, 0), (0, 1), (3, 0), (0, 3)]
    order = [(y, x, c) for y, x in far + near for c in (0, 1)] + [(0, 0, 1)]
    if peers != 32:
        order = [(0, 0, step) for step in range(1, peers)]
    return order


def kernel(
    groups,
    peers,
    cols_hbm,
    count_hbm,
    wanted_hbm,
    basis_hbm,
    tiles_hbm,
    out_hbm,
    cols,
    count,
    wanted,
    basis,
    tiles,
    inv_root,
    applied,
    out,
    own,
    stage,
    recv,
    rim,
    pieces,
    table,
    table_s,
    gram_near,
    gram_far,
    arg_sem,
    tile_sem,
    list_sem,
    send_sem,
    recv_sem,
    rim_send,
    rim_recv,
    near_sem,
    far_sem,
    out_sem,
):
    blocks, vectors, side = basis.shape
    half = vectors // HALVES
    per_row = cols.shape[1]
    group = lax.axis_index("group")
    me = lax.axis_index("row")
    up = lax.rem(group + 1, groups)
    down = lax.rem(group + groups - 1, groups)
    zero_slot = blocks + SLOTS * peers + 2 * RIM

    def peer(step):
        return lax.rem(me + step, peers)

    def offset_peer(offset):
        dy, dx, dc = offset
        if peers != 32:
            return peer(dc)
        y, x, c = me // 8, lax.rem(me // 2, 4), lax.rem(me, 2)
        return lax.rem(y + dy, 4) * 8 + lax.rem(x + dx, 4) * 2 + lax.rem(c + dc, 2)

    def far_peer(step):
        return lax.rem(group + step, groups)

    def remote(source, target, sems, group_to, row_to):
        return pltpu.make_async_remote_copy(
            src_ref=source,
            dst_ref=target,
            send_sem=sems[0],
            recv_sem=sems[1],
            device_id=(group_to, row_to),
            device_id_type=MESH,
        )

    def wait_for(ref, sem):
        pltpu.make_async_copy(ref, ref, sem).wait()

    def copy_in(b):
        return pltpu.make_async_copy(tiles_hbm.at[b], tiles.at[b], tile_sem.at[b])

    arguments = [
        pltpu.make_async_copy(source, target, arg_sem.at[i])
        for i, (source, target) in enumerate(
            (
                (wanted_hbm, wanted),
                (count_hbm, count),
                (basis_hbm, basis),
                (cols_hbm, cols),
            )
        )
    ]

    barrier = pltpu.get_barrier_semaphore()

    @pl.loop(1, peers)
    def _(step):
        pl.semaphore_signal(barrier, inc=1, device_id=(group, peer(step)), device_id_type=MESH)

    @pl.loop(1, groups)
    def _(step):
        pl.semaphore_signal(barrier, inc=1, device_id=(far_peer(step), me), device_id_type=MESH)

    for copy in arguments:
        copy.start()
    for b in range(blocks):
        copy_in(b).start()
    for copy in arguments:
        copy.wait()
    pl.semaphore_wait(barrier, peers - 1 + groups - 1)

    for offset in send_order(peers):
        remote(
            wanted, table.at[me], (list_sem.at[0], list_sem.at[1]), group, offset_peer(offset)
        ).start()

    ones = jnp.ones((vectors, 3 * side), BF16)

    @pl.loop(0, blocks)
    def _(b):
        copy_in(b).wait()
        live = count[b]
        total = jnp.zeros((side, side), F32)
        for s in range(per_row):
            wide = tiles[b, s].astype(F32)
            square = wide * wide
            if s >= MINLIVE:
                square = square * jnp.where(s < live, 1.0, 0.0).astype(F32)
            total = total + square
        sums = lax.dot_general(
            ones, jnp.concatenate(split(total, 3), axis=1), NT, preferred_element_type=F32
        )
        root = 1.0 / jnp.sqrt(jnp.sqrt(1e-06 + sums))
        inv_root[b] = root
        value = basis[b] * root
        for h in range(HALVES):
            own[0, h, b] = value[h * half : (h + 1) * half]

    pieces[zero_slot] = jnp.zeros(pieces.shape[1:], BF16)
    part = table.at[pl.ds(0, peers - 1)]
    wait_for(part, list_sem.at[0])
    wait_for(part, list_sem.at[1])
    to_scalar = pltpu.make_async_copy(table, table_s, arg_sem.at[0])
    to_scalar.start()
    to_scalar.wait()

    first_block = (group * peers + me) * blocks

    def send(t, h):
        for at, (lo, target) in enumerate(((blocks - RIM, up), (0, down))):
            remote(
                own.at[t, h, pl.ds(lo, RIM)],
                rim.at[t, h, at],
                (rim_send.at[t, h, at], rim_recv.at[t, h, at]),
                target,
                me,
            ).start()
        for offset in send_order(peers):
            q = offset_peer(offset)
            for c in range(SLOTS):
                pick = jnp.clip(table_s[q, c, me] - first_block, 0, blocks - 1)
                stage[t, h, q, c] = own[t, h, pick]
            remote(
                stage.at[t, h, q],
                recv.at[t, h, me],
                (send_sem.at[t, h], recv_sem.at[t, h]),
                group,
                q,
            ).start()

    def put_pieces(at, value):
        high = value.astype(BF16).astype(F32)
        rest = value - high
        middle = rest.astype(BF16).astype(F32)
        parts = [high, middle, rest - middle, jnp.zeros_like(value)]
        pieces[pl.ds(at, value.shape[0])] = jnp.concatenate(parts, axis=1).astype(BF16)

    def multiply(t, h):
        put_pieces(0, own[t, h])
        wait_for(recv.at[t, h, pl.ds(0, peers - 1)], recv_sem.at[t, h])

        @pl.loop(0, peers, unroll=UNROLL_PIECES)
        def _(q):
            put_pieces(blocks + SLOTS * q, recv[t, h, q])

        for at in range(2):
            wait_for(rim.at[t, h, at], rim_recv.at[t, h, at])
            put_pieces(blocks + SLOTS * peers + RIM * at, rim[t, h, at])

        @pl.loop(0, blocks, unroll=UNROLL)
        def _(b):
            live = count[b]
            picked = []
            for s in range(per_row):
                slot = cols[b, s]
                if s >= MINLIVE:
                    slot = jnp.where(s < live, slot, zero_slot)
                picked.append(pieces[slot])
            both = lax.dot_general(
                jnp.concatenate(picked, axis=1),
                jnp.concatenate([tiles[b, s] for s in range(per_row)], axis=1),
                NT,
                preferred_element_type=F32,
            )
            product = both[:half] + both[half : 2 * half] + both[2 * half : 3 * half]
            root = inv_root[b, :half]
            product = product * root
            applied[t, h, b] = product
            own[t + 1, h, b] = product * root

    def wide(ref):
        return jnp.concatenate(
            [
                jnp.concatenate([ref[h, b] for b in range(blocks)], axis=1)
                for h in range(HALVES)
            ],
            axis=0,
        )

    row_of = lax.broadcasted_iota(jnp.int32, (vectors, side), 0)
    lane_of = lax.broadcasted_iota(jnp.int32, (vectors, side), 1)
    own_lane = lax.rem(row_of, 8) == lane_of // vectors
    row_total = groups * peers * blocks * side

    def gram_start(t, value):
        gram = lax.dot_general(
            value,
            jnp.concatenate([value] * (side // vectors), axis=0),
            NT,
            precision=HIGHEST,
            preferred_element_type=F32,
        )
        packed = jnp.sum(jnp.where(own_lane, gram, 0.0).reshape(vectors // 8, 8, side), axis=1)
        gram_near[t, me] = packed

        @pl.loop(1, peers)
        def _(step):
            here = gram_near.at[t, me]
            remote(here, here, (near_sem.at[t, 0], near_sem.at[t, 1]), group, peer(step)).start()

    def gram_far_start(t):
        wait_for(gram_near.at[t, pl.ds(0, peers - 1)], near_sem.at[t, 1])
        gram_far[t, group] = jnp.sum(gram_near[t], axis=0)

        @pl.loop(1, groups)
        def _(step):
            here = gram_far.at[t, group]
            remote(here, here, (far_sem.at[t, 0], far_sem.at[t, 1]), far_peer(step), me).start()

    def gram_end(t):
        wait_for(gram_far.at[t, pl.ds(0, groups - 1)], far_sem.at[t, 1])
        packed = jnp.sum(gram_far[t], axis=0) / row_total
        rows = jnp.broadcast_to(packed[:, None, :], (vectors // 8, 8, side)).reshape(vectors, side)
        full = jnp.where(own_lane, rows, 0.0)
        for shift in (64, 32, 16):
            full = full + pltpu.roll(full, shift, 1)
        columns = [
            jnp.broadcast_to(full[:, k : k + 1], (vectors, side)) for k in range(vectors)
        ]
        inverse = jnp.where(lane_of == row_of, 1.0, 0.0).astype(F32)
        pivots = jnp.zeros((vectors, side), F32)

        def row(value, j):
            return jnp.broadcast_to(value[j : j + 1], (vectors, side))

        for j in range(vectors):
            pivot = row(columns[j], j)
            pivots = jnp.where(row_of == j, pivot, pivots)
            factor = jnp.where(row_of > j, columns[j] / pivot, 0.0)
            inverse = inverse - factor * row(inverse, j)
            for k in range(j + 1, vectors):
                columns[k] = columns[k] - factor * row(columns[k], j)
        return (inverse / jnp.sqrt(pivots))[:, :vectors]

    def normalise(inverse, value):
        return lax.dot_general(
            inverse,
            value,
            (((1,), (0,)), ((), ())),
            precision=HIGHEST,
            preferred_element_type=F32,
        )

    def copy_out(t):
        return pltpu.make_async_copy(out.at[t], out_hbm.at[t], out_sem.at[t])

    def store_out(t, value):
        for b in range(blocks):
            out[t, b] = value[:, b * side : (b + 1) * side]
        copy_out(t).start()

    @pl.loop(0, HALVES)
    def _(h):
        send(0, h)

    last = HALVES - 1

    @pl.loop(0, ITERS)
    def _(t):
        @pl.loop(0, HALVES)
        def _(h):
            @pl.when((t == 2) & (h == 0))
            def _():
                gram_far_start(1)

            multiply(t, h)

            @pl.when((t < ITERS - 1) & (h == last))
            def _():
                gram_start(t, wide(applied.at[t]))

            @pl.when(t < ITERS - 1)
            def _():
                send(t + 1, h)

            @pl.when((t == 1) & (h == 0))
            def _():
                gram_far_start(0)

            @pl.when((t == 1) & (h == last))
            def _():
                store_out(0, normalise(gram_end(0), wide(applied.at[0])))

    inverse = gram_end(1)
    third = normalise(inverse, wide(applied.at[2]))
    gram_start(2, third)
    store_out(1, normalise(inverse, wide(applied.at[1])))
    gram_far_start(2)
    store_out(2, normalise(gram_end(2), third))

    @pl.loop(0, ITERS)
    def _(t):
        for h in range(HALVES):
            wait_for(stage.at[t, h, pl.ds(0, peers - 1)], send_sem.at[t, h])
            for at in range(2):
                wait_for(rim.at[t, h, at], rim_send.at[t, h, at])
        wait_for(gram_near.at[t, pl.ds(0, peers - 1)], near_sem.at[t, 0])
        wait_for(gram_far.at[t, pl.ds(0, groups - 1)], far_sem.at[t, 0])

    for t in range(ITERS):
        copy_out(t).wait()


def local(groups, peers, start_basis, tiles, tile_cols, tile_count, recv_list):
    blocks, per_row, side, _ = tiles.shape
    vectors = start_basis.shape[1]
    half = vectors // HALVES
    wanted = jnp.transpose(recv_list.reshape(peers, SLOTS))
    slots = blocks + SLOTS * peers + 2 * RIM + 1
    dma = pltpu.SemaphoreType.DMA
    vmem = pltpu.VMEM
    out_shape = (ITERS, blocks, vectors, side)
    return pl.pallas_call(
        functools.partial(kernel, groups, peers),
        out_shape=jax.ShapeDtypeStruct(out_shape, F32),
        in_specs=[pl.BlockSpec(memory_space=pltpu.HBM)] * 5,
        out_specs=pl.BlockSpec(memory_space=pltpu.HBM),
        scratch_shapes=[
            pltpu.SMEM(tile_cols.shape, jnp.int32),
            pltpu.SMEM(tile_count.shape, jnp.int32),
            vmem(wanted.shape, jnp.int32),
            vmem((blocks, vectors, side), F32),
            vmem((blocks, per_row, side, side), BF16),
            vmem((blocks, vectors, side), F32),
            vmem((ITERS, HALVES, blocks, half, side), F32),
            vmem(out_shape, F32),
            vmem((ITERS + 1, HALVES, blocks, half, side), F32),
            vmem((ITERS, HALVES, peers, SLOTS, half, side), F32),
            vmem((ITERS, HALVES, peers, SLOTS, half, side), F32),
            vmem((ITERS, HALVES, 2, RIM, half, side), F32),
            vmem((slots, 4 * half, side), BF16),
            vmem((peers, SLOTS, peers), jnp.int32),
            pltpu.SMEM((peers, SLOTS, peers), jnp.int32),
            vmem((ITERS, peers, vectors // 8, side), F32),
            vmem((ITERS, groups, vectors // 8, side), F32),
            dma((4,)),
            dma((blocks,)),
            dma((2,)),
            dma((ITERS, HALVES)),
            dma((ITERS, HALVES)),
            dma((ITERS, HALVES, 2)),
            dma((ITERS, HALVES, 2)),
            dma((ITERS, 2)),
            dma((ITERS, 2)),
            dma((ITERS,)),
        ],
        compiler_params=pltpu.CompilerParams(
            collective_id=0, has_side_effects=True, vmem_limit_bytes=60 << 20
        ),
    )(tile_cols, tile_count, wanted, start_basis, tiles)


def solution(mesh):
    placed = (
        P(("group", "row"), None, None),
        P(("group", "row"), None, None, None),
        P(("group", "row"), None),
        P(("group", "row")),
        P("group", "row", None, None),
    )
    return jax.shard_map(
        functools.partial(local, mesh.shape["group"], mesh.shape["row"]),
        mesh=mesh,
        in_specs=placed,
        out_specs=P(None, ("group", "row"), None, None),
        check_vma=False,
    )
```

```python
import functools

import jax
import jax.numpy as jnp
from jax import lax
from jax.experimental import pallas as pl
from jax.experimental.pallas import tpu as pltpu
from jax.sharding import PartitionSpec as P

SLOTS = 2
RIM = 2
ITERS = 3
MINLIVE = 10
HALVES = 2
UNROLL = 8
UNROLL_PIECES = 8
MESH = pl.DeviceIdType.MESH
F32 = jnp.float32
BF16 = jnp.bfloat16
HIGHEST = lax.Precision.HIGHEST
NT = (((1,), (1,)), ((), ()))


def send_order(peers):
    far = [(2, 2), (1, 2), (2, 1), (3, 2), (2, 3), (1, 1), (3, 3), (1, 3), (3, 1)]
    near = [(2, 0), (0, 2), (1, 0), (0, 1), (3, 0), (0, 3)]
    order = [(y, x, c) for y, x in far + near for c in (0, 1)] + [(0, 0, 1)]
    if peers != 32:
        order = [(0, 0, step) for step in range(1, peers)]
    return order


def kernel(
    groups,
    peers,
    cols_hbm,
    count_hbm,
    wanted_hbm,
    basis_hbm,
    tiles_hbm,
    out,
    cols,
    count,
    wanted,
    basis,
    tiles_in,
    tiles,
    inv_root,
    applied,
    own,
    stage,
    recv,
    rim,
    pieces,
    table,
    table_s,
    gram_near,
    gram_far,
    arg_sem,
    tile_sem,
    list_sem,
    send_sem,
    recv_sem,
    rim_send,
    rim_recv,
    near_sem,
    far_sem,
):
    blocks, vectors, side = basis.shape
    half = vectors // HALVES
    per_row = cols.shape[1]
    group = lax.axis_index("group")
    me = lax.axis_index("row")
    up = lax.rem(group + 1, groups)
    down = lax.rem(group + groups - 1, groups)
    zero_slot = blocks + SLOTS * peers + 2 * RIM

    def peer(step):
        return lax.rem(me + step, peers)

    def offset_peer(offset):
        dy, dx, dc = offset
        if peers != 32:
            return peer(dc)
        y, x, c = me // 8, lax.rem(me // 2, 4), lax.rem(me, 2)
        return lax.rem(y + dy, 4) * 8 + lax.rem(x + dx, 4) * 2 + lax.rem(c + dc, 2)

    def far_peer(step):
        return lax.rem(group + step, groups)

    def remote(source, target, sems, group_to, row_to):
        return pltpu.make_async_remote_copy(
            src_ref=source,
            dst_ref=target,
            send_sem=sems[0],
            recv_sem=sems[1],
            device_id=(group_to, row_to),
            device_id_type=MESH,
        )

    def wait_for(ref, sem):
        pltpu.make_async_copy(ref, ref, sem).wait()

    def copy_in(b):
        return pltpu.make_async_copy(tiles_hbm.at[b], tiles_in.at[b], tile_sem.at[b])

    arguments = [
        pltpu.make_async_copy(source, target, arg_sem.at[i])
        for i, (source, target) in enumerate(
            (
                (wanted_hbm, wanted),
                (count_hbm, count),
                (basis_hbm, basis),
                (cols_hbm, cols),
            )
        )
    ]

    barrier = pltpu.get_barrier_semaphore()

    @pl.loop(1, peers)
    def _(step):
        pl.semaphore_signal(barrier, inc=1, device_id=(group, peer(step)), device_id_type=MESH)

    @pl.loop(1, groups)
    def _(step):
        pl.semaphore_signal(barrier, inc=1, device_id=(far_peer(step), me), device_id_type=MESH)

    for copy in arguments:
        copy.start()
    for b in range(blocks):
        copy_in(b).start()
    for copy in arguments:
        copy.wait()
    pl.semaphore_wait(barrier, peers - 1 + groups - 1)

    for offset in send_order(peers):
        remote(
            wanted, table.at[me], (list_sem.at[0], list_sem.at[1]), group, offset_peer(offset)
        ).start()

    @pl.loop(0, blocks)
    def _(b):
        copy_in(b).wait()
        live = count[b]
        total = jnp.zeros((side, side), F32)
        for s in range(per_row):
            turned = tiles_in[b, s].astype(F32).T
            tiles[b, s * side : (s + 1) * side] = turned.astype(BF16)
            square = turned * turned
            if s >= MINLIVE:
                square = square * jnp.where(s < live, 1.0, 0.0).astype(F32)
            total = total + square
        sums = jnp.broadcast_to(jnp.sum(total, axis=0, keepdims=True), (vectors, side))
        root = 1.0 / jnp.sqrt(jnp.sqrt(1e-06 + sums))
        inv_root[b] = root
        value = basis[b] * root
        for h in range(HALVES):
            own[0, h, b] = value[h * half : (h + 1) * half]

    pieces[zero_slot] = jnp.zeros(pieces.shape[1:], BF16)
    part = table.at[pl.ds(0, peers - 1)]
    wait_for(part, list_sem.at[0])
    wait_for(part, list_sem.at[1])
    to_scalar = pltpu.make_async_copy(table, table_s, arg_sem.at[0])
    to_scalar.start()
    to_scalar.wait()

    first_block = (group * peers + me) * blocks

    def send(t, h):
        for at, (lo, target) in enumerate(((blocks - RIM, up), (0, down))):
            remote(
                own.at[t, h, pl.ds(lo, RIM)],
                rim.at[t, h, at],
                (rim_send.at[t, h, at], rim_recv.at[t, h, at]),
                target,
                me,
            ).start()
        for offset in send_order(peers):
            q = offset_peer(offset)
            for c in range(SLOTS):
                pick = jnp.clip(table_s[q, c, me] - first_block, 0, blocks - 1)
                stage[t, h, q, c] = own[t, h, pick]
            remote(
                stage.at[t, h, q],
                recv.at[t, h, me],
                (send_sem.at[t, h], recv_sem.at[t, h]),
                group,
                q,
            ).start()

    def put_pieces(at, value):
        high = value.astype(BF16).astype(F32)
        rest = value - high
        middle = rest.astype(BF16).astype(F32)
        parts = [high, middle, rest - middle, jnp.zeros_like(value)]
        pieces[pl.ds(at, value.shape[0])] = jnp.concatenate(parts, axis=1).astype(BF16)

    def multiply(t, h):
        put_pieces(0, own[t, h])
        wait_for(recv.at[t, h, pl.ds(0, peers - 1)], recv_sem.at[t, h])

        @pl.loop(0, peers, unroll=UNROLL_PIECES)
        def _(q):
            put_pieces(blocks + SLOTS * q, recv[t, h, q])

        for at in range(2):
            wait_for(rim.at[t, h, at], rim_recv.at[t, h, at])
            put_pieces(blocks + SLOTS * peers + RIM * at, rim[t, h, at])

        @pl.loop(0, blocks, unroll=UNROLL)
        def _(b):
            live = count[b]
            picked = []
            for s in range(per_row):
                slot = cols[b, s]
                if s >= MINLIVE:
                    slot = jnp.where(s < live, slot, zero_slot)
                picked.append(pieces[slot])
            both = lax.dot_general(
                jnp.concatenate(picked, axis=1),
                tiles[b],
                (((1,), (0,)), ((), ())),
                preferred_element_type=F32,
            )
            product = both[:half] + both[half : 2 * half] + both[2 * half : 3 * half]
            root = inv_root[b, :half]
            product = product * root
            applied[t, h, b] = product
            own[t + 1, h, b] = product * root

    def wide(ref):
        return jnp.concatenate(
            [
                jnp.concatenate([ref[h, b] for b in range(blocks)], axis=1)
                for h in range(HALVES)
            ],
            axis=0,
        )

    row_of = lax.broadcasted_iota(jnp.int32, (vectors, side), 0)
    lane_of = lax.broadcasted_iota(jnp.int32, (vectors, side), 1)
    own_lane = lax.rem(row_of, 8) == lane_of // vectors
    row_total = groups * peers * blocks * side

    def gram_start(t, value):
        gram = lax.dot_general(
            value,
            jnp.concatenate([value] * (side // vectors), axis=0),
            NT,
            precision=HIGHEST,
            preferred_element_type=F32,
        )
        packed = jnp.sum(jnp.where(own_lane, gram, 0.0).reshape(vectors // 8, 8, side), axis=1)
        gram_near[t, me] = packed

        @pl.loop(1, peers)
        def _(step):
            here = gram_near.at[t, me]
            remote(here, here, (near_sem.at[t, 0], near_sem.at[t, 1]), group, peer(step)).start()

    def gram_far_start(t):
        wait_for(gram_near.at[t, pl.ds(0, peers - 1)], near_sem.at[t, 1])
        gram_far[t, group] = jnp.sum(gram_near[t], axis=0)

        @pl.loop(1, groups)
        def _(step):
            here = gram_far.at[t, group]
            remote(here, here, (far_sem.at[t, 0], far_sem.at[t, 1]), far_peer(step), me).start()

    def gram_end(t):
        wait_for(gram_far.at[t, pl.ds(0, groups - 1)], far_sem.at[t, 1])
        packed = jnp.sum(gram_far[t], axis=0) / row_total
        rows = jnp.broadcast_to(packed[:, None, :], (vectors // 8, 8, side)).reshape(vectors, side)
        full = jnp.where(own_lane, rows, 0.0)
        for shift in (64, 32, 16):
            full = full + pltpu.roll(full, shift, 1)
        columns = [
            jnp.broadcast_to(full[:, k : k + 1], (vectors, side)) for k in range(vectors)
        ]
        inverse = jnp.where(lane_of == row_of, 1.0, 0.0).astype(F32)
        pivots = jnp.zeros((vectors, side), F32)

        def row(value, j):
            return jnp.broadcast_to(value[j : j + 1], (vectors, side))

        for j in range(vectors):
            pivot = row(columns[j], j)
            pivots = jnp.where(row_of == j, pivot, pivots)
            factor = jnp.where(row_of > j, columns[j] / pivot, 0.0)
            inverse = inverse - factor * row(inverse, j)
            for k in range(j + 1, vectors):
                columns[k] = columns[k] - factor * row(columns[k], j)
        return (inverse / jnp.sqrt(pivots))[:, :vectors]

    def normalise(inverse, value):
        return lax.dot_general(
            inverse,
            value,
            (((1,), (0,)), ((), ())),
            precision=HIGHEST,
            preferred_element_type=F32,
        )

    def store_out(t, value):
        for b in range(blocks):
            out[t, b] = value[:, b * side : (b + 1) * side]

    @pl.loop(0, HALVES)
    def _(h):
        send(0, h)

    last = HALVES - 1

    @pl.loop(0, ITERS)
    def _(t):
        @pl.loop(0, HALVES)
        def _(h):
            @pl.when((t == 2) & (h == 0))
            def _():
                gram_far_start(1)

            multiply(t, h)

            @pl.when((t < ITERS - 1) & (h == last))
            def _():
                gram_start(t, wide(applied.at[t]))

            @pl.when(t < ITERS - 1)
            def _():
                send(t + 1, h)

            @pl.when((t == 1) & (h == 0))
            def _():
                gram_far_start(0)

            @pl.when((t == 1) & (h == last))
            def _():
                store_out(0, normalise(gram_end(0), wide(applied.at[0])))

    inverse = gram_end(1)
    third = normalise(inverse, wide(applied.at[2]))
    gram_start(2, third)
    store_out(1, normalise(inverse, wide(applied.at[1])))
    gram_far_start(2)
    store_out(2, normalise(gram_end(2), third))

    @pl.loop(0, ITERS)
    def _(t):
        for h in range(HALVES):
            wait_for(stage.at[t, h, pl.ds(0, peers - 1)], send_sem.at[t, h])
            for at in range(2):
                wait_for(rim.at[t, h, at], rim_send.at[t, h, at])
        wait_for(gram_near.at[t, pl.ds(0, peers - 1)], near_sem.at[t, 0])
        wait_for(gram_far.at[t, pl.ds(0, groups - 1)], far_sem.at[t, 0])


def local(groups, peers, start_basis, tiles, tile_cols, tile_count, recv_list):
    blocks, per_row, side, _ = tiles.shape
    vectors = start_basis.shape[1]
    half = vectors // HALVES
    wanted = jnp.transpose(recv_list.reshape(peers, SLOTS))
    slots = blocks + SLOTS * peers + 2 * RIM + 1
    dma = pltpu.SemaphoreType.DMA
    vmem = pltpu.VMEM
    out_shape = (ITERS, blocks, vectors, side)
    operands = (tile_cols, tile_count, wanted, start_basis, tiles)
    return pl.pallas_call(
        functools.partial(kernel, groups, peers),
        out_shape=jax.ShapeDtypeStruct(out_shape, F32),
        in_specs=[pl.BlockSpec(memory_space=pltpu.HBM)] * 5,
        out_specs=pl.BlockSpec(memory_space=pltpu.VMEM),
        scratch_shapes=[
            pltpu.SMEM(tile_cols.shape, jnp.int32),
            pltpu.SMEM(tile_count.shape, jnp.int32),
            vmem(wanted.shape, jnp.int32),
            vmem((blocks, vectors, side), F32),
            vmem((blocks, per_row, side, side), BF16),
            vmem((blocks, per_row * side, side), BF16),
            vmem((blocks, vectors, side), F32),
            vmem((ITERS, HALVES, blocks, half, side), F32),
            vmem((ITERS + 1, HALVES, blocks, half, side), F32),
            vmem((ITERS, HALVES, peers, SLOTS, half, side), F32),
            vmem((ITERS, HALVES, peers, SLOTS, half, side), F32),
            vmem((ITERS, HALVES, 2, RIM, half, side), F32),
            vmem((slots, 4 * half, side), BF16),
            vmem((peers, SLOTS, peers), jnp.int32),
            pltpu.SMEM((peers, SLOTS, peers), jnp.int32),
            vmem((ITERS, peers, vectors // 8, side), F32),
            vmem((ITERS, groups, vectors // 8, side), F32),
            dma((4,)),
            dma((blocks,)),
            dma((2,)),
            dma((ITERS, HALVES)),
            dma((ITERS, HALVES)),
            dma((ITERS, HALVES, 2)),
            dma((ITERS, HALVES, 2)),
            dma((ITERS, 2)),
            dma((ITERS, 2)),
        ],
        compiler_params=pltpu.CompilerParams(
            collective_id=0, has_side_effects=True, vmem_limit_bytes=32 << 20
        ),
    )(*[pltpu.with_memory_space_constraint(value, pltpu.HBM) for value in operands])


def solution(mesh):
    placed = (
        P(("group", "row"), None, None),
        P(("group", "row"), None, None, None),
        P(("group", "row"), None),
        P(("group", "row")),
        P("group", "row", None, None),
    )
    return jax.shard_map(
        functools.partial(local, mesh.shape["group"], mesh.shape["row"]),
        mesh=mesh,
        in_specs=placed,
        out_specs=P(None, ("group", "row"), None, None),
        check_vma=False,
    )
```

```python
import functools

import jax
import jax.numpy as jnp
from jax import lax
from jax.experimental import pallas as pl
from jax.experimental.pallas import tpu as pltpu
from jax.sharding import PartitionSpec as P

SLOTS = 2
RIM = 2
ITERS = 3
MINLIVE = 10
HALVES = 2
UNROLL = 8
UNROLL_PIECES = 8
MESH = pl.DeviceIdType.MESH
F32 = jnp.float32
BF16 = jnp.bfloat16
HIGHEST = lax.Precision.HIGHEST
NT = (((1,), (1,)), ((), ()))


def split(x, count):
    parts = []
    for _ in range(count):
        parts.append(x.astype(BF16))
        x = x - parts[-1].astype(F32)
    return parts


def send_order(peers):
    far = [(2, 2), (1, 2), (2, 1), (3, 2), (2, 3), (1, 1), (3, 3), (1, 3), (3, 1)]
    near = [(2, 0), (0, 2), (1, 0), (0, 1), (3, 0), (0, 3)]
    order = [(y, x, c) for y, x in far + near for c in (0, 1)] + [(0, 0, 1)]
    if peers != 32:
        order = [(0, 0, step) for step in range(1, peers)]
    return order


def kernel(
    groups,
    peers,
    cols_hbm,
    count_hbm,
    wanted_hbm,
    basis_hbm,
    tiles_hbm,
    out,
    cols,
    count,
    wanted,
    basis,
    tiles_in,
    tiles,
    inv_root,
    applied,
    own,
    stage,
    recv,
    rim,
    pieces,
    table,
    table_s,
    gram_near,
    gram_far,
    first_inverse,
    arg_sem,
    tile_sem,
    list_sem,
    send_sem,
    recv_sem,
    rim_send,
    rim_recv,
    near_sem,
    far_sem,
):
    blocks, vectors, side = basis.shape
    half = vectors // HALVES
    per_row = cols.shape[1]
    group = lax.axis_index("group")
    me = lax.axis_index("row")
    up = lax.rem(group + 1, groups)
    down = lax.rem(group + groups - 1, groups)
    zero_slot = blocks + SLOTS * peers + 2 * RIM

    def peer(step):
        return lax.rem(me + step, peers)

    def offset_peer(offset):
        dy, dx, dc = offset
        if peers != 32:
            return peer(dc)
        y, x, c = me // 8, lax.rem(me // 2, 4), lax.rem(me, 2)
        return lax.rem(y + dy, 4) * 8 + lax.rem(x + dx, 4) * 2 + lax.rem(c + dc, 2)

    def far_peer(step):
        return lax.rem(group + step, groups)

    def remote(source, target, sems, group_to, row_to):
        return pltpu.make_async_remote_copy(
            src_ref=source,
            dst_ref=target,
            send_sem=sems[0],
            recv_sem=sems[1],
            device_id=(group_to, row_to),
            device_id_type=MESH,
        )

    def wait_for(ref, sem):
        pltpu.make_async_copy(ref, ref, sem).wait()

    def copy_in(b):
        return pltpu.make_async_copy(tiles_hbm.at[b], tiles_in.at[b], tile_sem.at[b])

    arguments = [
        pltpu.make_async_copy(source, target, arg_sem.at[i])
        for i, (source, target) in enumerate(
            (
                (wanted_hbm, wanted),
                (count_hbm, count),
                (basis_hbm, basis),
                (cols_hbm, cols),
            )
        )
    ]

    barrier = pltpu.get_barrier_semaphore()

    for step in sorted(range(1, groups), key=lambda step: -min(step, groups - step)):
        pl.semaphore_signal(barrier, inc=1, device_id=(far_peer(step), me), device_id_type=MESH)
    for offset in send_order(peers):
        q = offset_peer(offset)
        pl.semaphore_signal(barrier, inc=1, device_id=(group, q), device_id_type=MESH)

    for copy in arguments:
        copy.start()
    for b in range(blocks):
        copy_in(b).start()
    for copy in arguments:
        copy.wait()
    pl.semaphore_wait(barrier, peers - 1 + groups - 1)

    for offset in send_order(peers):
        remote(
            wanted, table.at[me], (list_sem.at[0], list_sem.at[1]), group, offset_peer(offset)
        ).start()

    @pl.loop(0, blocks)
    def _(b):
        copy_in(b).wait()
        live = count[b]
        total = jnp.zeros((side, side), F32)
        for s in range(per_row):
            turned = tiles_in[b, s].astype(F32).T
            tiles[b, s * side : (s + 1) * side] = turned.astype(BF16)
            square = turned * turned
            if s >= MINLIVE:
                square = square * jnp.where(s < live, 1.0, 0.0).astype(F32)
            total = total + square
        sums = jnp.broadcast_to(jnp.sum(total, axis=0, keepdims=True), (vectors, side))
        root = 1.0 / jnp.sqrt(jnp.sqrt(1e-06 + sums))
        inv_root[b] = root
        value = basis[b] * root
        for h in range(HALVES):
            own[0, h, b] = value[h * half : (h + 1) * half]

    pieces[zero_slot] = jnp.zeros(pieces.shape[1:], BF16)
    part = table.at[pl.ds(0, peers - 1)]
    wait_for(part, list_sem.at[1])
    to_scalar = pltpu.make_async_copy(table, table_s, arg_sem.at[0])
    to_scalar.start()
    to_scalar.wait()

    first_block = (group * peers + me) * blocks

    def send(t, h):
        for at, (lo, target) in enumerate(((blocks - RIM, up), (0, down))):
            remote(
                own.at[t, h, pl.ds(lo, RIM)],
                rim.at[t, h, at],
                (rim_send.at[t, h, at], rim_recv.at[t, h, at]),
                target,
                me,
            ).start()
        for offset in send_order(peers):
            q = offset_peer(offset)
            for c in range(SLOTS):
                pick = jnp.clip(table_s[q, c, me] - first_block, 0, blocks - 1)
                stage[t, h, q, c] = own[t, h, pick]
            remote(
                stage.at[t, h, q],
                recv.at[t, h, me],
                (send_sem.at[t, h], recv_sem.at[t, h]),
                group,
                q,
            ).start()

    def put_pieces(at, value):
        high = value.astype(BF16).astype(F32)
        rest = value - high
        middle = rest.astype(BF16).astype(F32)
        parts = [high, middle, rest - middle, jnp.zeros_like(value)]
        pieces[pl.ds(at, value.shape[0])] = jnp.concatenate(parts, axis=1).astype(BF16)

    def multiply(t, h):
        put_pieces(0, own[t, h])
        wait_for(recv.at[t, h, pl.ds(0, peers - 1)], recv_sem.at[t, h])

        @pl.loop(0, peers, unroll=UNROLL_PIECES)
        def _(q):
            put_pieces(blocks + SLOTS * q, recv[t, h, q])

        for at in range(2):
            wait_for(rim.at[t, h, at], rim_recv.at[t, h, at])
            put_pieces(blocks + SLOTS * peers + RIM * at, rim[t, h, at])

        @pl.loop(0, blocks, unroll=UNROLL)
        def _(b):
            live = count[b]
            picked = []
            for s in range(per_row):
                slot = cols[b, s]
                if s >= MINLIVE:
                    slot = jnp.where(s < live, slot, zero_slot)
                picked.append(pieces[slot])
            both = lax.dot_general(
                jnp.concatenate(picked, axis=1),
                tiles[b],
                (((1,), (0,)), ((), ())),
                preferred_element_type=F32,
            )
            product = both[:half] + both[half : 2 * half] + both[2 * half : 3 * half]
            root = inv_root[b, :half]
            product = product * root
            applied[t, h, b] = product
            own[t + 1, h, b] = product * root

    def wide(ref):
        return jnp.concatenate(
            [
                jnp.concatenate([ref[h, b] for b in range(blocks)], axis=1)
                for h in range(HALVES)
            ],
            axis=0,
        )

    row_of = lax.broadcasted_iota(jnp.int32, (vectors, side), 0)
    lane_of = lax.broadcasted_iota(jnp.int32, (vectors, side), 1)
    own_lane = lax.rem(row_of, 8) == lane_of // vectors
    row_total = groups * peers * blocks * side

    def gram_start(t, value):
        parts = split(value, 3)
        all_parts = jnp.concatenate(parts, axis=0)
        products = jnp.zeros((3 * vectors, side), F32)
        for part in reversed(parts):
            products = products + lax.dot_general(
                all_parts,
                jnp.concatenate([part] * (side // vectors), axis=0),
                NT,
                preferred_element_type=F32,
            )
        gram = products[2 * vectors :] + products[vectors : 2 * vectors] + products[:vectors]
        packed = jnp.sum(jnp.where(own_lane, gram, 0.0).reshape(vectors // 8, 8, side), axis=1)
        gram_far[t, group] = packed

        @pl.loop(1, groups)
        def _(step):
            here = gram_far.at[t, group]
            remote(here, here, (far_sem.at[t, 0], far_sem.at[t, 1]), far_peer(step), me).start()

    def gram_near_start(t):
        wait_for(gram_far.at[t, pl.ds(0, groups - 1)], far_sem.at[t, 1])
        gram_near[t, me] = jnp.sum(gram_far[t], axis=0)

        for offset in send_order(peers):
            here = gram_near.at[t, me]
            sems = (near_sem.at[t, 0], near_sem.at[t, 1])
            remote(here, here, sems, group, offset_peer(offset)).start()

    def gram_end(t):
        wait_for(gram_near.at[t, pl.ds(0, peers - 1)], near_sem.at[t, 1])
        packed = jnp.sum(gram_near[t], axis=0) / row_total
        rows = jnp.broadcast_to(packed[:, None, :], (vectors // 8, 8, side)).reshape(vectors, side)
        full = jnp.where(own_lane, rows, 0.0)
        for shift in (64, 32, 16):
            full = full + pltpu.roll(full, shift, 1)
        columns = [
            jnp.broadcast_to(full[:, k : k + 1], (vectors, side)) for k in range(vectors)
        ]
        inverse = jnp.where(lane_of == row_of, 1.0, 0.0).astype(F32)
        pivots = jnp.zeros((vectors, side), F32)

        def row(value, j):
            return jnp.broadcast_to(value[j : j + 1], (vectors, side))

        for j in range(vectors):
            pivot = row(columns[j], j)
            pivots = jnp.where(row_of == j, pivot, pivots)
            factor = jnp.where(row_of > j, columns[j] / pivot, 0.0)
            inverse = inverse - factor * row(inverse, j)
            for k in range(j + 1, vectors):
                columns[k] = columns[k] - factor * row(columns[k], j)
        return (inverse / jnp.sqrt(pivots))[:, :vectors]

    def normalise(inverse, value):
        return lax.dot_general(
            inverse,
            value,
            (((1,), (0,)), ((), ())),
            precision=HIGHEST,
            preferred_element_type=F32,
        )

    def store_out(t, value):
        for b in range(blocks):
            out[t, b] = value[:, b * side : (b + 1) * side]

    @pl.loop(0, HALVES)
    def _(h):
        send(0, h)

    last = HALVES - 1

    @pl.loop(0, ITERS)
    def _(t):
        @pl.loop(0, HALVES)
        def _(h):
            @pl.when((t == 1) & (h == 0))
            def _():
                gram_near_start(0)

            @pl.when((t == 2) & (h == last))
            def _():
                gram_near_start(1)
                first_inverse[...] = gram_end(0)

            multiply(t, h)

            @pl.when((t < ITERS - 1) & (h == last))
            def _():
                gram_start(t, wide(applied.at[t]))

            @pl.when(t < ITERS - 1)
            def _():
                send(t + 1, h)

    third = normalise(first_inverse[...], wide(applied.at[2]))
    gram_start(2, third)
    store_out(0, normalise(first_inverse[...], wide(applied.at[0])))
    gram_near_start(2)
    store_out(1, normalise(gram_end(1), wide(applied.at[1])))
    store_out(2, normalise(gram_end(2), third))

    wait_for(part, list_sem.at[0])

    @pl.loop(0, ITERS)
    def _(t):
        for h in range(HALVES):
            wait_for(stage.at[t, h, pl.ds(0, peers - 1)], send_sem.at[t, h])
            for at in range(2):
                wait_for(rim.at[t, h, at], rim_send.at[t, h, at])
        wait_for(gram_near.at[t, pl.ds(0, peers - 1)], near_sem.at[t, 0])
        wait_for(gram_far.at[t, pl.ds(0, groups - 1)], far_sem.at[t, 0])


def local(groups, peers, start_basis, tiles, tile_cols, tile_count, recv_list):
    blocks, per_row, side, _ = tiles.shape
    vectors = start_basis.shape[1]
    half = vectors // HALVES
    wanted = jnp.transpose(recv_list.reshape(peers, SLOTS))
    slots = blocks + SLOTS * peers + 2 * RIM + 1
    dma = pltpu.SemaphoreType.DMA
    vmem = pltpu.VMEM
    out_shape = (ITERS, blocks, vectors, side)
    operands = (tile_cols, tile_count, wanted, start_basis, tiles)
    return pl.pallas_call(
        functools.partial(kernel, groups, peers),
        out_shape=jax.ShapeDtypeStruct(out_shape, F32),
        in_specs=[pl.BlockSpec(memory_space=pltpu.HBM)] * 5,
        out_specs=pl.BlockSpec(memory_space=pltpu.VMEM),
        scratch_shapes=[
            pltpu.SMEM(tile_cols.shape, jnp.int32),
            pltpu.SMEM(tile_count.shape, jnp.int32),
            vmem(wanted.shape, jnp.int32),
            vmem((blocks, vectors, side), F32),
            vmem((blocks, per_row, side, side), BF16),
            vmem((blocks, per_row * side, side), BF16),
            vmem((blocks, vectors, side), F32),
            vmem((ITERS, HALVES, blocks, half, side), F32),
            vmem((ITERS + 1, HALVES, blocks, half, side), F32),
            vmem((ITERS, HALVES, peers, SLOTS, half, side), F32),
            vmem((ITERS, HALVES, peers, SLOTS, half, side), F32),
            vmem((ITERS, HALVES, 2, RIM, half, side), F32),
            vmem((slots, 4 * half, side), BF16),
            vmem((peers, SLOTS, peers), jnp.int32),
            pltpu.SMEM((peers, SLOTS, peers), jnp.int32),
            vmem((ITERS, peers, vectors // 8, side), F32),
            vmem((ITERS, groups, vectors // 8, side), F32),
            vmem((vectors, vectors), F32),
            dma((4,)),
            dma((blocks,)),
            dma((2,)),
            dma((ITERS, HALVES)),
            dma((ITERS, HALVES)),
            dma((ITERS, HALVES, 2)),
            dma((ITERS, HALVES, 2)),
            dma((ITERS, 2)),
            dma((ITERS, 2)),
        ],
        compiler_params=pltpu.CompilerParams(
            collective_id=0, has_side_effects=True, vmem_limit_bytes=32 << 20
        ),
    )(*[pltpu.with_memory_space_constraint(value, pltpu.HBM) for value in operands])


def solution(mesh):
    placed = (
        P(("group", "row"), None, None),
        P(("group", "row"), None, None, None),
        P(("group", "row"), None),
        P(("group", "row")),
        P("group", "row", None, None),
    )
    return jax.shard_map(
        functools.partial(local, mesh.shape["group"], mesh.shape["row"]),
        mesh=mesh,
        in_specs=placed,
        out_specs=P(None, ("group", "row"), None, None),
        check_vma=False,
    )
```

```python
import functools

import jax
import jax.numpy as jnp
from jax import lax
from jax.experimental import pallas as pl
from jax.experimental.pallas import tpu as pltpu
from jax.sharding import PartitionSpec as P

SLOTS = 2
RIM = 2
ITERS = 3
MINLIVE = 10
HALVES = 2
UNROLL = 8
UNROLL_PIECES = 8
MESH = pl.DeviceIdType.MESH
F32 = jnp.float32
BF16 = jnp.bfloat16
HIGHEST = lax.Precision.HIGHEST
NT = (((1,), (1,)), ((), ()))


def split(x, count):
    parts = []
    for _ in range(count):
        parts.append(x.astype(BF16))
        x = x - parts[-1].astype(F32)
    return parts


def send_order(peers):
    far = [(2, 2), (1, 2), (2, 1), (3, 2), (2, 3), (1, 1), (3, 3), (1, 3), (3, 1)]
    near = [(2, 0), (0, 2), (1, 0), (0, 1), (3, 0), (0, 3)]
    order = [(y, x, c) for c in (0, 1) for y, x in far + near] + [(0, 0, 1)]
    if peers != 32:
        order = [(0, 0, step) for step in range(1, peers)]
    return order


def kernel(
    groups,
    peers,
    cols_hbm,
    count_hbm,
    wanted_hbm,
    basis_hbm,
    tiles_hbm,
    out,
    cols,
    count,
    wanted,
    basis,
    tiles_in,
    tiles,
    inv_root,
    applied,
    own,
    stage,
    recv,
    rim,
    pieces,
    table,
    table_s,
    gram_near,
    gram_far,
    first_inverse,
    arg_sem,
    tile_sem,
    list_sem,
    send_sem,
    recv_sem,
    rim_send,
    rim_recv,
    near_sem,
    far_sem,
):
    blocks, vectors, side = basis.shape
    half = vectors // HALVES
    per_row = cols.shape[1]
    group = lax.axis_index("group")
    me = lax.axis_index("row")
    up = lax.rem(group + 1, groups)
    down = lax.rem(group + groups - 1, groups)
    zero_slot = blocks + SLOTS * peers + 2 * RIM

    def peer(step):
        return lax.rem(me + step, peers)

    def offset_peer(offset):
        dy, dx, dc = offset
        if peers != 32:
            return peer(dc)
        y, x, c = me // 8, lax.rem(me // 2, 4), lax.rem(me, 2)
        return lax.rem(y + dy, 4) * 8 + lax.rem(x + dx, 4) * 2 + lax.rem(c + dc, 2)

    def far_peer(step):
        return lax.rem(group + step, groups)

    def remote(source, target, sems, group_to, row_to):
        return pltpu.make_async_remote_copy(
            src_ref=source,
            dst_ref=target,
            send_sem=sems[0],
            recv_sem=sems[1],
            device_id=(group_to, row_to),
            device_id_type=MESH,
        )

    def wait_for(ref, sem):
        pltpu.make_async_copy(ref, ref, sem).wait()

    def copy_in(b):
        return pltpu.make_async_copy(tiles_hbm.at[b], tiles_in.at[b], tile_sem.at[b])

    arguments = [
        pltpu.make_async_copy(source, target, arg_sem.at[i])
        for i, (source, target) in enumerate(
            (
                (wanted_hbm, wanted),
                (count_hbm, count),
                (basis_hbm, basis),
                (cols_hbm, cols),
            )
        )
    ]

    barrier = pltpu.get_barrier_semaphore()

    for step in sorted(range(1, groups), key=lambda step: -min(step, groups - step)):
        pl.semaphore_signal(barrier, inc=1, device_id=(far_peer(step), me), device_id_type=MESH)
    for offset in send_order(peers):
        q = offset_peer(offset)
        pl.semaphore_signal(barrier, inc=1, device_id=(group, q), device_id_type=MESH)

    for copy in arguments:
        copy.start()
    for b in range(blocks):
        copy_in(b).start()
    for copy in arguments:
        copy.wait()
    pl.semaphore_wait(barrier, peers - 1 + groups - 1)

    for offset in send_order(peers):
        remote(
            wanted, table.at[me], (list_sem.at[0], list_sem.at[1]), group, offset_peer(offset)
        ).start()

    @pl.loop(0, blocks)
    def _(b):
        copy_in(b).wait()
        live = count[b]
        total = jnp.zeros((side, side), F32)
        for s in range(per_row):
            turned = tiles_in[b, s].astype(F32).T
            tiles[b, s * side : (s + 1) * side] = turned.astype(BF16)
            square = turned * turned
            if s >= MINLIVE:
                square = square * jnp.where(s < live, 1.0, 0.0).astype(F32)
            total = total + square
        sums = jnp.broadcast_to(jnp.sum(total, axis=0, keepdims=True), (vectors, side))
        root = 1.0 / jnp.sqrt(jnp.sqrt(1e-06 + sums))
        inv_root[b] = root
        value = basis[b] * root
        for h in range(HALVES):
            own[0, h, b] = value[h * half : (h + 1) * half]

    pieces[zero_slot] = jnp.zeros(pieces.shape[1:], BF16)
    part = table.at[pl.ds(0, peers - 1)]
    wait_for(part, list_sem.at[1])
    to_scalar = pltpu.make_async_copy(table, table_s, arg_sem.at[0])
    to_scalar.start()
    to_scalar.wait()

    first_block = (group * peers + me) * blocks

    def send(t, h):
        for at, (lo, target) in enumerate(((blocks - RIM, up), (0, down))):
            remote(
                own.at[t, h, pl.ds(lo, RIM)],
                rim.at[t, h, at],
                (rim_send.at[t, h, at], rim_recv.at[t, h, at]),
                target,
                me,
            ).start()
        for offset in send_order(peers):
            q = offset_peer(offset)
            for c in range(SLOTS):
                pick = jnp.clip(table_s[q, c, me] - first_block, 0, blocks - 1)
                stage[t, h, q, c] = own[t, h, pick]
            remote(
                stage.at[t, h, q],
                recv.at[t, h, me],
                (send_sem.at[t, h], recv_sem.at[t, h]),
                group,
                q,
            ).start()

    def put_pieces(at, value):
        high = value.astype(BF16).astype(F32)
        rest = value - high
        middle = rest.astype(BF16).astype(F32)
        parts = [high, middle, rest - middle, jnp.zeros_like(value)]
        pieces[pl.ds(at, value.shape[0])] = jnp.concatenate(parts, axis=1).astype(BF16)

    def multiply(t, h):
        put_pieces(0, own[t, h])
        wait_for(recv.at[t, h, pl.ds(0, peers - 1)], recv_sem.at[t, h])

        @pl.loop(0, peers, unroll=UNROLL_PIECES)
        def _(q):
            put_pieces(blocks + SLOTS * q, recv[t, h, q])

        for at in range(2):
            wait_for(rim.at[t, h, at], rim_recv.at[t, h, at])
            put_pieces(blocks + SLOTS * peers + RIM * at, rim[t, h, at])

        @pl.loop(0, blocks, unroll=UNROLL)
        def _(b):
            live = count[b]
            picked = []
            for s in range(per_row):
                slot = cols[b, s]
                if s >= MINLIVE:
                    slot = jnp.where(s < live, slot, zero_slot)
                picked.append(pieces[slot])
            both = lax.dot_general(
                jnp.concatenate(picked, axis=1),
                tiles[b],
                (((1,), (0,)), ((), ())),
                preferred_element_type=F32,
            )
            product = both[:half] + both[half : 2 * half] + both[2 * half : 3 * half]
            root = inv_root[b, :half]
            product = product * root
            applied[t, h, b] = product
            own[t + 1, h, b] = product * root

    def wide(ref):
        return jnp.concatenate(
            [
                jnp.concatenate([ref[h, b] for b in range(blocks)], axis=1)
                for h in range(HALVES)
            ],
            axis=0,
        )

    row_of = lax.broadcasted_iota(jnp.int32, (vectors, side), 0)
    lane_of = lax.broadcasted_iota(jnp.int32, (vectors, side), 1)
    own_lane = lax.rem(row_of, 8) == lane_of // vectors
    row_total = groups * peers * blocks * side

    def gram_start(t, value):
        parts = split(value, 3)
        all_parts = jnp.concatenate(parts, axis=0)
        products = jnp.zeros((3 * vectors, side), F32)
        for part in reversed(parts):
            products = products + lax.dot_general(
                all_parts,
                jnp.concatenate([part] * (side // vectors), axis=0),
                NT,
                preferred_element_type=F32,
            )
        gram = products[2 * vectors :] + products[vectors : 2 * vectors] + products[:vectors]
        packed = jnp.sum(jnp.where(own_lane, gram, 0.0).reshape(vectors // 8, 8, side), axis=1)
        gram_far[t, group] = packed

        @pl.loop(1, groups)
        def _(step):
            here = gram_far.at[t, group]
            remote(here, here, (far_sem.at[t, 0], far_sem.at[t, 1]), far_peer(step), me).start()

    def gram_near_start(t):
        wait_for(gram_far.at[t, pl.ds(0, groups - 1)], far_sem.at[t, 1])
        gram_near[t, me] = jnp.sum(gram_far[t], axis=0)

        for offset in send_order(peers):
            here = gram_near.at[t, me]
            sems = (near_sem.at[t, 0], near_sem.at[t, 1])
            remote(here, here, sems, group, offset_peer(offset)).start()

    def gram_end(t):
        wait_for(gram_near.at[t, pl.ds(0, peers - 1)], near_sem.at[t, 1])
        packed = jnp.sum(gram_near[t], axis=0) / row_total
        rows = jnp.broadcast_to(packed[:, None, :], (vectors // 8, 8, side)).reshape(vectors, side)
        full = jnp.where(own_lane, rows, 0.0)
        for shift in (64, 32, 16):
            full = full + pltpu.roll(full, shift, 1)
        columns = [
            jnp.broadcast_to(full[:, k : k + 1], (vectors, side)) for k in range(vectors)
        ]
        inverse = jnp.where(lane_of == row_of, 1.0, 0.0).astype(F32)
        pivots = jnp.zeros((vectors, side), F32)

        def row(value, j):
            return jnp.broadcast_to(value[j : j + 1], (vectors, side))

        for j in range(vectors):
            pivot = row(columns[j], j)
            pivots = jnp.where(row_of == j, pivot, pivots)
            factor = jnp.where(row_of > j, columns[j] / pivot, 0.0)
            inverse = inverse - factor * row(inverse, j)
            for k in range(j + 1, vectors):
                columns[k] = columns[k] - factor * row(columns[k], j)
        return (inverse / jnp.sqrt(pivots))[:, :vectors]

    def normalise(inverse, value):
        return lax.dot_general(
            inverse,
            value,
            (((1,), (0,)), ((), ())),
            precision=HIGHEST,
            preferred_element_type=F32,
        )

    def store_out(t, value):
        for b in range(blocks):
            out[t, b] = value[:, b * side : (b + 1) * side]

    @pl.loop(0, HALVES)
    def _(h):
        send(0, h)

    last = HALVES - 1

    @pl.loop(0, ITERS)
    def _(t):
        @pl.loop(0, HALVES)
        def _(h):
            @pl.when((t == 1) & (h == 0))
            def _():
                gram_near_start(0)

            @pl.when((t == 2) & (h == last))
            def _():
                gram_near_start(1)
                first_inverse[...] = gram_end(0)

            multiply(t, h)

            @pl.when((t < ITERS - 1) & (h == last))
            def _():
                gram_start(t, wide(applied.at[t]))

            @pl.when(t < ITERS - 1)
            def _():
                send(t + 1, h)

    third = normalise(first_inverse[...], wide(applied.at[2]))
    gram_start(2, third)
    store_out(0, normalise(first_inverse[...], wide(applied.at[0])))
    gram_near_start(2)
    store_out(1, normalise(gram_end(1), wide(applied.at[1])))
    store_out(2, normalise(gram_end(2), third))

    wait_for(part, list_sem.at[0])

    @pl.loop(0, ITERS)
    def _(t):
        for h in range(HALVES):
            wait_for(stage.at[t, h, pl.ds(0, peers - 1)], send_sem.at[t, h])
            for at in range(2):
                wait_for(rim.at[t, h, at], rim_send.at[t, h, at])
        wait_for(gram_near.at[t, pl.ds(0, peers - 1)], near_sem.at[t, 0])
        wait_for(gram_far.at[t, pl.ds(0, groups - 1)], far_sem.at[t, 0])


def local(groups, peers, start_basis, tiles, tile_cols, tile_count, recv_list):
    blocks, per_row, side, _ = tiles.shape
    vectors = start_basis.shape[1]
    half = vectors // HALVES
    wanted = jnp.transpose(recv_list.reshape(peers, SLOTS))
    slots = blocks + SLOTS * peers + 2 * RIM + 1
    dma = pltpu.SemaphoreType.DMA
    vmem = pltpu.VMEM
    out_shape = (ITERS, blocks, vectors, side)
    operands = (tile_cols, tile_count, wanted, start_basis, tiles)
    return pl.pallas_call(
        functools.partial(kernel, groups, peers),
        out_shape=jax.ShapeDtypeStruct(out_shape, F32),
        in_specs=[pl.BlockSpec(memory_space=pltpu.HBM)] * 5,
        out_specs=pl.BlockSpec(memory_space=pltpu.VMEM),
        scratch_shapes=[
            pltpu.SMEM(tile_cols.shape, jnp.int32),
            pltpu.SMEM(tile_count.shape, jnp.int32),
            vmem(wanted.shape, jnp.int32),
            vmem((blocks, vectors, side), F32),
            vmem((blocks, per_row, side, side), BF16),
            vmem((blocks, per_row * side, side), BF16),
            vmem((blocks, vectors, side), F32),
            vmem((ITERS, HALVES, blocks, half, side), F32),
            vmem((ITERS + 1, HALVES, blocks, half, side), F32),
            vmem((ITERS, HALVES, peers, SLOTS, half, side), F32),
            vmem((ITERS, HALVES, peers, SLOTS, half, side), F32),
            vmem((ITERS, HALVES, 2, RIM, half, side), F32),
            vmem((slots, 4 * half, side), BF16),
            vmem((peers, SLOTS, peers), jnp.int32),
            pltpu.SMEM((peers, SLOTS, peers), jnp.int32),
            vmem((ITERS, peers, vectors // 8, side), F32),
            vmem((ITERS, groups, vectors // 8, side), F32),
            vmem((vectors, vectors), F32),
            dma((4,)),
            dma((blocks,)),
            dma((2,)),
            dma((ITERS, HALVES)),
            dma((ITERS, HALVES)),
            dma((ITERS, HALVES, 2)),
            dma((ITERS, HALVES, 2)),
            dma((ITERS, 2)),
            dma((ITERS, 2)),
        ],
        compiler_params=pltpu.CompilerParams(
            collective_id=0, has_side_effects=True, vmem_limit_bytes=32 << 20
        ),
    )(*[pltpu.with_memory_space_constraint(value, pltpu.HBM) for value in operands])


def solution(mesh):
    placed = (
        P(("group", "row"), None, None),
        P(("group", "row"), None, None, None),
        P(("group", "row"), None),
        P(("group", "row")),
        P("group", "row", None, None),
    )
    return jax.shard_map(
        functools.partial(local, mesh.shape["group"], mesh.shape["row"]),
        mesh=mesh,
        in_specs=placed,
        out_specs=P(None, ("group", "row"), None, None),
        check_vma=False,
    )
```

```python
import functools

import jax
import jax.numpy as jnp
from jax import lax
from jax.experimental import pallas as pl
from jax.experimental.pallas import tpu as pltpu
from jax.sharding import PartitionSpec as P

SLOTS = 2
RIM = 2
ITERS = 3
MINLIVE = 10
HALVES = 2
UNROLL = 8
UNROLL_PIECES = 8
MESH = pl.DeviceIdType.MESH
F32 = jnp.float32
BF16 = jnp.bfloat16
HIGHEST = lax.Precision.HIGHEST
NT = (((1,), (1,)), ((), ()))


def split(x, count):
    parts = []
    for _ in range(count):
        parts.append(x.astype(BF16))
        x = x - parts[-1].astype(F32)
    return parts


def send_order(peers):
    far = [(2, 2), (1, 2), (2, 1), (3, 2), (2, 3), (1, 1), (3, 3), (1, 3), (3, 1)]
    near = [(2, 0), (0, 2), (1, 0), (0, 1), (3, 0), (0, 3)]
    order = [(y, x, c) for c in (0, 1) for y, x in far + near] + [(0, 0, 1)]
    if peers != 32:
        order = [(0, 0, step) for step in range(1, peers)]
    return order


def kernel(
    groups,
    peers,
    cols_hbm,
    count_hbm,
    wanted_hbm,
    basis_hbm,
    tiles_hbm,
    out,
    cols,
    count,
    wanted,
    basis,
    tiles_in,
    tiles,
    inv_root,
    applied,
    own,
    stage,
    recv,
    rim,
    pieces,
    table,
    table_s,
    gram_near,
    gram_far,
    first_inverse,
    arg_sem,
    tile_sem,
    list_sem,
    send_sem,
    recv_sem,
    rim_send,
    rim_recv,
    near_sem,
    far_sem,
):
    blocks, vectors, side = basis.shape
    half = vectors // HALVES
    per_row = cols.shape[1]
    group = lax.axis_index("group")
    me = lax.axis_index("row")
    up = lax.rem(group + 1, groups)
    down = lax.rem(group + groups - 1, groups)
    zero_slot = blocks + SLOTS * peers + 2 * RIM

    def peer(step):
        return lax.rem(me + step, peers)

    def offset_peer(offset):
        dy, dx, dc = offset
        if peers != 32:
            return peer(dc)
        y, x, c = me // 8, lax.rem(me // 2, 4), lax.rem(me, 2)
        return lax.rem(y + dy, 4) * 8 + lax.rem(x + dx, 4) * 2 + lax.rem(c + dc, 2)

    def far_peer(step):
        return lax.rem(group + step, groups)

    def remote(source, target, sems, group_to, row_to):
        return pltpu.make_async_remote_copy(
            src_ref=source,
            dst_ref=target,
            send_sem=sems[0],
            recv_sem=sems[1],
            device_id=(group_to, row_to),
            device_id_type=MESH,
        )

    def wait_for(ref, sem):
        pltpu.make_async_copy(ref, ref, sem).wait()

    def copy_in(b):
        return pltpu.make_async_copy(tiles_hbm.at[b], tiles_in.at[b], tile_sem.at[b])

    arguments = [
        pltpu.make_async_copy(source, target, arg_sem.at[i])
        for i, (source, target) in enumerate(
            (
                (wanted_hbm, wanted),
                (count_hbm, count),
                (basis_hbm, basis),
                (cols_hbm, cols),
            )
        )
    ]

    barrier = pltpu.get_barrier_semaphore()

    for step in sorted(range(1, groups), key=lambda step: -min(step, groups - step)):
        pl.semaphore_signal(barrier, inc=1, device_id=(far_peer(step), me), device_id_type=MESH)
    for offset in send_order(peers):
        q = offset_peer(offset)
        pl.semaphore_signal(barrier, inc=1, device_id=(group, q), device_id_type=MESH)

    for copy in arguments:
        copy.start()
    for b in range(blocks):
        copy_in(b).start()
    for copy in arguments:
        copy.wait()
    pl.semaphore_wait(barrier, peers - 1 + groups - 1)

    for offset in send_order(peers):
        remote(
            wanted, table.at[me], (list_sem.at[0], list_sem.at[1]), group, offset_peer(offset)
        ).start()

    @pl.loop(0, blocks)
    def _(b):
        copy_in(b).wait()
        live = count[b]
        total = jnp.zeros((side, side), F32)
        for s in range(per_row):
            turned = tiles_in[b, s].astype(F32).T
            tiles[b, s * side : (s + 1) * side] = turned.astype(BF16)
            square = turned * turned
            if s >= MINLIVE:
                square = square * jnp.where(s < live, 1.0, 0.0).astype(F32)
            total = total + square
        sums = jnp.broadcast_to(jnp.sum(total, axis=0, keepdims=True), (vectors, side))
        root = 1.0 / jnp.sqrt(jnp.sqrt(1e-06 + sums))
        inv_root[b] = root
        value = basis[b] * root
        for h in range(HALVES):
            own[0, h, b] = value[h * half : (h + 1) * half]

    pieces[zero_slot] = jnp.zeros(pieces.shape[1:], BF16)
    part = table.at[pl.ds(0, peers - 1)]
    wait_for(part, list_sem.at[1])
    to_scalar = pltpu.make_async_copy(table, table_s, arg_sem.at[0])
    to_scalar.start()
    to_scalar.wait()

    first_block = (group * peers + me) * blocks

    def send(t, h):
        for at, (lo, target) in enumerate(((blocks - RIM, up), (0, down))):
            remote(
                own.at[t, h, pl.ds(lo, RIM)],
                rim.at[t, h, at],
                (rim_send.at[t, h, at], rim_recv.at[t, h, at]),
                target,
                me,
            ).start()
        for offset in send_order(peers):
            q = offset_peer(offset)
            for c in range(SLOTS):
                pick = jnp.clip(table_s[q, c, me] - first_block, 0, blocks - 1)
                stage[t, h, q, c] = own[t, h, pick]
            remote(
                stage.at[t, h, q],
                recv.at[t, h, me],
                (send_sem.at[t, h], recv_sem.at[t, h]),
                group,
                q,
            ).start()

    def put_pieces(at, value):
        high = value.astype(BF16).astype(F32)
        rest = value - high
        middle = rest.astype(BF16).astype(F32)
        parts = [high, middle, rest - middle, jnp.zeros_like(value)]
        pieces[pl.ds(at, value.shape[0])] = jnp.concatenate(parts, axis=1).astype(BF16)

    def multiply(t, h):
        put_pieces(0, own[t, h])
        wait_for(recv.at[t, h, pl.ds(0, peers - 1)], recv_sem.at[t, h])

        @pl.loop(0, peers, unroll=UNROLL_PIECES)
        def _(q):
            put_pieces(blocks + SLOTS * q, recv[t, h, q])

        for at in range(2):
            wait_for(rim.at[t, h, at], rim_recv.at[t, h, at])
            put_pieces(blocks + SLOTS * peers + RIM * at, rim[t, h, at])

        @pl.loop(0, blocks, unroll=UNROLL)
        def _(b):
            live = count[b]
            picked = []
            for s in range(per_row):
                slot = cols[b, s]
                if s >= MINLIVE:
                    slot = jnp.where(s < live, slot, zero_slot)
                picked.append(pieces[slot])
            both = lax.dot_general(
                jnp.concatenate(picked, axis=1),
                tiles[b],
                (((1,), (0,)), ((), ())),
                preferred_element_type=F32,
            )
            product = both[:half] + both[half : 2 * half] + both[2 * half : 3 * half]
            root = inv_root[b, :half]
            product = product * root
            applied[t, h, b] = product
            own[t + 1, h, b] = product * root

    def wide(ref):
        return jnp.concatenate(
            [
                jnp.concatenate([ref[h, b] for b in range(blocks)], axis=1)
                for h in range(HALVES)
            ],
            axis=0,
        )

    row_of = lax.broadcasted_iota(jnp.int32, (vectors, side), 0)
    lane_of = lax.broadcasted_iota(jnp.int32, (vectors, side), 1)
    own_lane = lax.rem(row_of, 8) == lane_of // vectors
    row_total = groups * peers * blocks * side

    def gram_start(t, value):
        parts = split(value, 3)
        all_parts = jnp.concatenate(parts, axis=0)
        products = jnp.zeros((3 * vectors, side), F32)
        for part in reversed(parts):
            products = products + lax.dot_general(
                all_parts,
                jnp.concatenate([part] * (side // vectors), axis=0),
                NT,
                preferred_element_type=F32,
            )
        gram = products[2 * vectors :] + products[vectors : 2 * vectors] + products[:vectors]
        packed = jnp.sum(jnp.where(own_lane, gram, 0.0).reshape(vectors // 8, 8, side), axis=1)
        gram_far[t, group] = packed

        @pl.loop(1, groups)
        def _(step):
            here = gram_far.at[t, group]
            remote(here, here, (far_sem.at[t, 0], far_sem.at[t, 1]), far_peer(step), me).start()

    def gram_near_start(t):
        wait_for(gram_far.at[t, pl.ds(0, groups - 1)], far_sem.at[t, 1])
        gram_near[t, me] = jnp.sum(gram_far[t], axis=0)

        for offset in send_order(peers):
            here = gram_near.at[t, me]
            sems = (near_sem.at[t, 0], near_sem.at[t, 1])
            remote(here, here, sems, group, offset_peer(offset)).start()

    def gram_end(t):
        wait_for(gram_near.at[t, pl.ds(0, peers - 1)], near_sem.at[t, 1])
        packed = jnp.sum(gram_near[t], axis=0) / row_total
        rows = jnp.broadcast_to(packed[:, None, :], (vectors // 8, 8, side)).reshape(vectors, side)
        full = jnp.where(own_lane, rows, 0.0)
        for shift in (64, 32, 16):
            full = full + pltpu.roll(full, shift, 1)
        columns = [
            jnp.broadcast_to(full[:, k : k + 1], (vectors, side)) for k in range(vectors)
        ]
        inverse = jnp.where(lane_of == row_of, 1.0, 0.0).astype(F32)
        pivots = jnp.zeros((vectors, side), F32)

        def row(value, j):
            return jnp.broadcast_to(value[j : j + 1], (vectors, side))

        for j in range(vectors):
            pivot = row(columns[j], j)
            pivots = jnp.where(row_of == j, pivot, pivots)
            factor = jnp.where(row_of > j, columns[j] / pivot, 0.0)
            inverse = inverse - factor * row(inverse, j)
            for k in range(j + 1, vectors):
                columns[k] = columns[k] - factor * row(columns[k], j)
        return (inverse / jnp.sqrt(pivots))[:, :vectors]

    def normalise(inverse, value):
        return lax.dot_general(
            inverse,
            value,
            (((1,), (0,)), ((), ())),
            precision=HIGHEST,
            preferred_element_type=F32,
        )

    def store_out(t, value):
        for b in range(blocks):
            out[t, b] = value[:, b * side : (b + 1) * side]

    @pl.loop(0, HALVES)
    def _(h):
        send(0, h)

    last = HALVES - 1

    @pl.loop(0, ITERS)
    def _(t):
        @pl.loop(0, HALVES)
        def _(h):
            @pl.when((t == 1) & (h == last))
            def _():
                gram_near_start(0)

            @pl.when((t == 2) & (h == last))
            def _():
                first_inverse[...] = gram_end(0)

            multiply(t, h)

            @pl.when(t < ITERS - 1)
            def _():
                send(t + 1, h)

            @pl.when((t < ITERS - 1) & (h == last))
            def _():
                gram_start(t, wide(applied.at[t]))

    third = normalise(first_inverse[...], wide(applied.at[2]))
    gram_start(2, third)
    gram_near_start(1)
    store_out(0, normalise(first_inverse[...], wide(applied.at[0])))
    gram_near_start(2)
    store_out(1, normalise(gram_end(1), wide(applied.at[1])))
    store_out(2, normalise(gram_end(2), third))

    wait_for(part, list_sem.at[0])

    @pl.loop(0, ITERS)
    def _(t):
        for h in range(HALVES):
            wait_for(stage.at[t, h, pl.ds(0, peers - 1)], send_sem.at[t, h])
            for at in range(2):
                wait_for(rim.at[t, h, at], rim_send.at[t, h, at])
        wait_for(gram_near.at[t, pl.ds(0, peers - 1)], near_sem.at[t, 0])
        wait_for(gram_far.at[t, pl.ds(0, groups - 1)], far_sem.at[t, 0])


def local(groups, peers, start_basis, tiles, tile_cols, tile_count, recv_list):
    blocks, per_row, side, _ = tiles.shape
    vectors = start_basis.shape[1]
    half = vectors // HALVES
    wanted = jnp.transpose(recv_list.reshape(peers, SLOTS))
    slots = blocks + SLOTS * peers + 2 * RIM + 1
    dma = pltpu.SemaphoreType.DMA
    vmem = pltpu.VMEM
    out_shape = (ITERS, blocks, vectors, side)
    operands = (tile_cols, tile_count, wanted, start_basis, tiles)
    return pl.pallas_call(
        functools.partial(kernel, groups, peers),
        out_shape=jax.ShapeDtypeStruct(out_shape, F32),
        in_specs=[pl.BlockSpec(memory_space=pltpu.HBM)] * 5,
        out_specs=pl.BlockSpec(memory_space=pltpu.VMEM),
        scratch_shapes=[
            pltpu.SMEM(tile_cols.shape, jnp.int32),
            pltpu.SMEM(tile_count.shape, jnp.int32),
            vmem(wanted.shape, jnp.int32),
            vmem((blocks, vectors, side), F32),
            vmem((blocks, per_row, side, side), BF16),
            vmem((blocks, per_row * side, side), BF16),
            vmem((blocks, vectors, side), F32),
            vmem((ITERS, HALVES, blocks, half, side), F32),
            vmem((ITERS + 1, HALVES, blocks, half, side), F32),
            vmem((ITERS, HALVES, peers, SLOTS, half, side), F32),
            vmem((ITERS, HALVES, peers, SLOTS, half, side), F32),
            vmem((ITERS, HALVES, 2, RIM, half, side), F32),
            vmem((slots, 4 * half, side), BF16),
            vmem((peers, SLOTS, peers), jnp.int32),
            pltpu.SMEM((peers, SLOTS, peers), jnp.int32),
            vmem((ITERS, peers, vectors // 8, side), F32),
            vmem((ITERS, groups, vectors // 8, side), F32),
            vmem((vectors, vectors), F32),
            dma((4,)),
            dma((blocks,)),
            dma((2,)),
            dma((ITERS, HALVES)),
            dma((ITERS, HALVES)),
            dma((ITERS, HALVES, 2)),
            dma((ITERS, HALVES, 2)),
            dma((ITERS, 2)),
            dma((ITERS, 2)),
        ],
        compiler_params=pltpu.CompilerParams(
            collective_id=0, has_side_effects=True, vmem_limit_bytes=32 << 20
        ),
    )(*[pltpu.with_memory_space_constraint(value, pltpu.HBM) for value in operands])


def solution(mesh):
    placed = (
        P(("group", "row"), None, None),
        P(("group", "row"), None, None, None),
        P(("group", "row"), None),
        P(("group", "row")),
        P("group", "row", None, None),
    )
    return jax.shard_map(
        functools.partial(local, mesh.shape["group"], mesh.shape["row"]),
        mesh=mesh,
        in_specs=placed,
        out_specs=P(None, ("group", "row"), None, None),
        check_vma=False,
    )
```

```python
import functools

import jax
import jax.numpy as jnp
from jax import lax
from jax.experimental import pallas as pl
from jax.experimental.pallas import tpu as pltpu
from jax.sharding import PartitionSpec as P

SLOTS = 2
RIM = 2
ITERS = 3
MINLIVE = 10
HALVES = 2
UNROLL = 8
UNROLL_PIECES = 8
MESH = pl.DeviceIdType.MESH
F32 = jnp.float32
BF16 = jnp.bfloat16
HIGHEST = lax.Precision.HIGHEST
NT = (((1,), (1,)), ((), ()))


def split(x, count):
    parts = []
    for _ in range(count):
        parts.append(x.astype(BF16))
        x = x - parts[-1].astype(F32)
    return parts


def send_order(peers):
    far = [(2, 2), (1, 2), (2, 1), (3, 2), (2, 3), (1, 1), (3, 3), (1, 3), (3, 1)]
    near = [(2, 0), (0, 2), (1, 0), (0, 1), (3, 0), (0, 3)]
    order = [(y, x, c) for c in (0, 1) for y, x in far + near] + [(0, 0, 1)]
    if peers != 32:
        order = [(0, 0, step) for step in range(1, peers)]
    return order


def kernel(
    groups,
    peers,
    cols_hbm,
    count_hbm,
    wanted_hbm,
    basis_hbm,
    tiles_hbm,
    out,
    cols,
    count,
    wanted,
    basis,
    tiles_in,
    tiles,
    inv_root,
    applied,
    own,
    stage,
    recv,
    rim,
    pieces,
    table,
    table_s,
    gram_near,
    gram_far,
    first_inverse,
    arg_sem,
    tile_sem,
    list_sem,
    send_sem,
    recv_sem,
    rim_send,
    rim_recv,
    near_sem,
    far_sem,
):
    blocks, vectors, side = basis.shape
    half = vectors // HALVES
    per_row = cols.shape[1]
    group = lax.axis_index("group")
    me = lax.axis_index("row")
    up = lax.rem(group + 1, groups)
    down = lax.rem(group + groups - 1, groups)
    zero_slot = blocks + SLOTS * peers + 2 * RIM

    def peer(step):
        return lax.rem(me + step, peers)

    def offset_peer(offset):
        dy, dx, dc = offset
        if peers != 32:
            return peer(dc)
        y, x, c = me // 8, lax.rem(me // 2, 4), lax.rem(me, 2)
        return lax.rem(y + dy, 4) * 8 + lax.rem(x + dx, 4) * 2 + lax.rem(c + dc, 2)

    def far_peer(step):
        return lax.rem(group + step, groups)

    def remote(source, target, sems, group_to, row_to):
        return pltpu.make_async_remote_copy(
            src_ref=source,
            dst_ref=target,
            send_sem=sems[0],
            recv_sem=sems[1],
            device_id=(group_to, row_to),
            device_id_type=MESH,
        )

    def wait_for(ref, sem):
        pltpu.make_async_copy(ref, ref, sem).wait()

    def copy_in(b):
        return pltpu.make_async_copy(tiles_hbm.at[b], tiles_in.at[b], tile_sem.at[b])

    arguments = [
        pltpu.make_async_copy(source, target, arg_sem.at[i])
        for i, (source, target) in enumerate(
            (
                (wanted_hbm, wanted),
                (count_hbm, count),
                (basis_hbm, basis),
                (cols_hbm, cols),
            )
        )
    ]

    barrier = pltpu.get_barrier_semaphore()

    for step in sorted(range(1, groups), key=lambda step: -min(step, groups - step)):
        pl.semaphore_signal(barrier, inc=1, device_id=(far_peer(step), me), device_id_type=MESH)
    for offset in send_order(peers):
        q = offset_peer(offset)
        pl.semaphore_signal(barrier, inc=1, device_id=(group, q), device_id_type=MESH)

    for copy in arguments:
        copy.start()
    for b in range(blocks):
        copy_in(b).start()
    for copy in arguments:
        copy.wait()
    pl.semaphore_wait(barrier, peers - 1 + groups - 1)

    for offset in send_order(peers):
        remote(
            wanted, table.at[me], (list_sem.at[0], list_sem.at[1]), group, offset_peer(offset)
        ).start()

    @pl.loop(0, blocks)
    def _(b):
        copy_in(b).wait()
        live = count[b]
        total = jnp.zeros((side, side), F32)
        for s in range(per_row):
            turned = tiles_in[b, s].astype(F32).T
            tiles[b, s * side : (s + 1) * side] = turned.astype(BF16)
            square = turned * turned
            if s >= MINLIVE:
                square = square * jnp.where(s < live, 1.0, 0.0).astype(F32)
            total = total + square
        sums = jnp.broadcast_to(jnp.sum(total, axis=0, keepdims=True), (vectors, side))
        root = 1.0 / jnp.sqrt(jnp.sqrt(1e-06 + sums))
        inv_root[b] = root
        value = basis[b] * root
        for h in range(HALVES):
            own[0, h, b] = value[h * half : (h + 1) * half]

    pieces[zero_slot] = jnp.zeros(pieces.shape[1:], BF16)
    part = table.at[pl.ds(0, peers - 1)]
    wait_for(part, list_sem.at[1])
    to_scalar = pltpu.make_async_copy(table, table_s, arg_sem.at[0])
    to_scalar.start()
    to_scalar.wait()

    first_block = (group * peers + me) * blocks

    def send(t, h):
        for at, (lo, target) in enumerate(((blocks - RIM, up), (0, down))):
            remote(
                own.at[t, h, pl.ds(lo, RIM)],
                rim.at[t, h, at],
                (rim_send.at[t, h, at], rim_recv.at[t, h, at]),
                target,
                me,
            ).start()
        for offset in send_order(peers):
            q = offset_peer(offset)
            for c in range(SLOTS):
                pick = jnp.clip(table_s[q, c, me] - first_block, 0, blocks - 1)
                stage[t, h, q, c] = own[t, h, pick]
            remote(
                stage.at[t, h, q],
                recv.at[t, h, me],
                (send_sem.at[t, h], recv_sem.at[t, h]),
                group,
                q,
            ).start()

    def put_pieces(at, value):
        high = value.astype(BF16).astype(F32)
        rest = value - high
        middle = rest.astype(BF16).astype(F32)
        parts = [high, middle, rest - middle, jnp.zeros_like(value)]
        pieces[pl.ds(at, value.shape[0])] = jnp.concatenate(parts, axis=1).astype(BF16)

    def multiply(t, h):
        put_pieces(0, own[t, h])
        wait_for(recv.at[t, h, pl.ds(0, peers - 1)], recv_sem.at[t, h])

        @pl.loop(0, peers, unroll=UNROLL_PIECES)
        def _(q):
            put_pieces(blocks + SLOTS * q, recv[t, h, q])

        for at in range(2):
            wait_for(rim.at[t, h, at], rim_recv.at[t, h, at])
            put_pieces(blocks + SLOTS * peers + RIM * at, rim[t, h, at])

        @pl.loop(0, blocks, unroll=UNROLL)
        def _(b):
            live = count[b]
            picked = []
            for s in range(per_row):
                slot = cols[b, s]
                if s >= MINLIVE:
                    slot = jnp.where(s < live, slot, zero_slot)
                picked.append(pieces[slot])
            both = lax.dot_general(
                jnp.concatenate(picked, axis=1),
                tiles[b],
                (((1,), (0,)), ((), ())),
                preferred_element_type=F32,
            )
            product = both[:half] + both[half : 2 * half] + both[2 * half : 3 * half]
            root = inv_root[b, :half]
            product = product * root
            applied[t, h, b] = product
            own[t + 1, h, b] = product * root

    def wide(ref):
        return jnp.concatenate(
            [
                jnp.concatenate([ref[h, b] for b in range(blocks)], axis=1)
                for h in range(HALVES)
            ],
            axis=0,
        )

    row_of = lax.broadcasted_iota(jnp.int32, (vectors, side), 0)
    lane_of = lax.broadcasted_iota(jnp.int32, (vectors, side), 1)
    own_lane = lax.rem(row_of, 8) == lane_of // vectors
    row_total = groups * peers * blocks * side

    def gram_start(t, value):
        parts = split(value, 3)
        all_parts = jnp.concatenate(parts, axis=0)
        products = jnp.zeros((3 * vectors, side), F32)
        for part in reversed(parts):
            products = products + lax.dot_general(
                all_parts,
                jnp.concatenate([part] * (side // vectors), axis=0),
                NT,
                preferred_element_type=F32,
            )
        gram = products[2 * vectors :] + products[vectors : 2 * vectors] + products[:vectors]
        packed = jnp.sum(jnp.where(own_lane, gram, 0.0).reshape(vectors // 8, 8, side), axis=1)
        gram_far[t, group] = packed

        for step in sorted(range(1, groups), key=lambda step: -min(step, groups - step)):
            here = gram_far.at[t, group]
            remote(here, here, (far_sem.at[t, 0], far_sem.at[t, 1]), far_peer(step), me).start()

    def gram_near_start(t):
        wait_for(gram_far.at[t, pl.ds(0, groups - 1)], far_sem.at[t, 1])
        gram_near[t, me] = jnp.sum(gram_far[t], axis=0)

        for offset in send_order(peers):
            here = gram_near.at[t, me]
            sems = (near_sem.at[t, 0], near_sem.at[t, 1])
            remote(here, here, sems, group, offset_peer(offset)).start()

    def gram_end(t):
        wait_for(gram_near.at[t, pl.ds(0, peers - 1)], near_sem.at[t, 1])
        packed = jnp.sum(gram_near[t], axis=0) / row_total
        rows = jnp.broadcast_to(packed[:, None, :], (vectors // 8, 8, side)).reshape(vectors, side)
        full = jnp.where(own_lane, rows, 0.0)
        for shift in (64, 32, 16):
            full = full + pltpu.roll(full, shift, 1)
        columns = [
            jnp.broadcast_to(full[:, k : k + 1], (vectors, side)) for k in range(vectors)
        ]
        inverse = jnp.where(lane_of == row_of, 1.0, 0.0).astype(F32)
        pivots = jnp.zeros((vectors, side), F32)

        def row(value, j):
            return jnp.broadcast_to(value[j : j + 1], (vectors, side))

        for j in range(vectors):
            pivot = row(columns[j], j)
            pivots = jnp.where(row_of == j, pivot, pivots)
            factor = jnp.where(row_of > j, columns[j] / pivot, 0.0)
            inverse = inverse - factor * row(inverse, j)
            for k in range(j + 1, vectors):
                columns[k] = columns[k] - factor * row(columns[k], j)
        return (inverse / jnp.sqrt(pivots))[:, :vectors]

    def normalise(inverse, value):
        return lax.dot_general(
            inverse,
            value,
            (((1,), (0,)), ((), ())),
            precision=HIGHEST,
            preferred_element_type=F32,
        )

    def store_out(t, value):
        for b in range(blocks):
            out[t, b] = value[:, b * side : (b + 1) * side]

    @pl.loop(0, HALVES)
    def _(h):
        send(0, h)

    last = HALVES - 1

    @pl.loop(0, ITERS)
    def _(t):
        @pl.loop(0, HALVES)
        def _(h):
            @pl.when((t == 1) & (h == last))
            def _():
                gram_near_start(0)

            @pl.when((t == 2) & (h == last))
            def _():
                first_inverse[...] = gram_end(0)

            multiply(t, h)

            @pl.when(t < ITERS - 1)
            def _():
                send(t + 1, h)

            @pl.when((t < ITERS - 1) & (h == last))
            def _():
                gram_start(t, wide(applied.at[t]))

    third = normalise(first_inverse[...], wide(applied.at[2]))
    gram_start(2, third)
    gram_near_start(1)
    store_out(0, normalise(first_inverse[...], wide(applied.at[0])))
    gram_near_start(2)
    store_out(1, normalise(gram_end(1), wide(applied.at[1])))
    store_out(2, normalise(gram_end(2), third))

    wait_for(part, list_sem.at[0])

    @pl.loop(0, ITERS)
    def _(t):
        for h in range(HALVES):
            wait_for(stage.at[t, h, pl.ds(0, peers - 1)], send_sem.at[t, h])
            for at in range(2):
                wait_for(rim.at[t, h, at], rim_send.at[t, h, at])
        wait_for(gram_near.at[t, pl.ds(0, peers - 1)], near_sem.at[t, 0])
        wait_for(gram_far.at[t, pl.ds(0, groups - 1)], far_sem.at[t, 0])


def local(groups, peers, start_basis, tiles, tile_cols, tile_count, recv_list):
    blocks, per_row, side, _ = tiles.shape
    vectors = start_basis.shape[1]
    half = vectors // HALVES
    wanted = jnp.transpose(recv_list.reshape(peers, SLOTS))
    slots = blocks + SLOTS * peers + 2 * RIM + 1
    dma = pltpu.SemaphoreType.DMA
    vmem = pltpu.VMEM
    out_shape = (ITERS, blocks, vectors, side)
    operands = (tile_cols, tile_count, wanted, start_basis, tiles)
    return pl.pallas_call(
        functools.partial(kernel, groups, peers),
        out_shape=jax.ShapeDtypeStruct(out_shape, F32),
        in_specs=[pl.BlockSpec(memory_space=pltpu.HBM)] * 5,
        out_specs=pl.BlockSpec(memory_space=pltpu.VMEM),
        scratch_shapes=[
            pltpu.SMEM(tile_cols.shape, jnp.int32),
            pltpu.SMEM(tile_count.shape, jnp.int32),
            vmem(wanted.shape, jnp.int32),
            vmem((blocks, vectors, side), F32),
            vmem((blocks, per_row, side, side), BF16),
            vmem((blocks, per_row * side, side), BF16),
            vmem((blocks, vectors, side), F32),
            vmem((ITERS, HALVES, blocks, half, side), F32),
            vmem((ITERS + 1, HALVES, blocks, half, side), F32),
            vmem((ITERS, HALVES, peers, SLOTS, half, side), F32),
            vmem((ITERS, HALVES, peers, SLOTS, half, side), F32),
            vmem((ITERS, HALVES, 2, RIM, half, side), F32),
            vmem((slots, 4 * half, side), BF16),
            vmem((peers, SLOTS, peers), jnp.int32),
            pltpu.SMEM((peers, SLOTS, peers), jnp.int32),
            vmem((ITERS, peers, vectors // 8, side), F32),
            vmem((ITERS, groups, vectors // 8, side), F32),
            vmem((vectors, vectors), F32),
            dma((4,)),
            dma((blocks,)),
            dma((2,)),
            dma((ITERS, HALVES)),
            dma((ITERS, HALVES)),
            dma((ITERS, HALVES, 2)),
            dma((ITERS, HALVES, 2)),
            dma((ITERS, 2)),
            dma((ITERS, 2)),
        ],
        compiler_params=pltpu.CompilerParams(
            collective_id=0, has_side_effects=True, vmem_limit_bytes=32 << 20
        ),
    )(*[pltpu.with_memory_space_constraint(value, pltpu.HBM) for value in operands])


def solution(mesh):
    placed = (
        P(("group", "row"), None, None),
        P(("group", "row"), None, None, None),
        P(("group", "row"), None),
        P(("group", "row")),
        P("group", "row", None, None),
    )
    return jax.shard_map(
        functools.partial(local, mesh.shape["group"], mesh.shape["row"]),
        mesh=mesh,
        in_specs=placed,
        out_specs=P(None, ("group", "row"), None, None),
        check_vma=False,
    )
```
